128 devices in a mesh: dp: 4 (over x_lo, core), expert: 32 (over y, z, x_hi).
Axes of the slice: x: 4 (x_hi: 2, x_lo: 2; x = x_hi * 2 + x_lo), y: 4, z: 4, core: 2. Of those that a mesh axis runs over, the one named last changes fastest.
Arguments:
- tokens: bfloat16 [16384, 3584], P(('dp', 'expert')), may hold values from -6 to 6
- cotangent: bfloat16 [16384, 3584], P(('dp', 'expert')), may hold values from -6 to 6
- expert_ids: int32 [16384, 2], P(('dp', 'expert')), may hold values from 0 to 31, all different within a row; in each aligned block of 128 rows (0 to 127, 128 to 255, ...) at most 12 rows name the same one
- combine: float32 [16384, 2], P(('dp', 'expert')), may hold values from 0.2 to 1
- slot_expert: int32 [32], replicated, may hold values from 0 to 31, each once
- swap_flag: int32 [32], replicated, may hold values from 0 to 1, as said below
- w_gate_up: bfloat16 [32, 2, 3584, 1024], P('expert', None, None, 'dp'), may hold values from -0.09375 to 0.09375
- w_down: bfloat16 [32, 1024, 3584], P('expert', 'dp'), may hold values from -0.1875 to 0.1875
- first_gate_up: bfloat16 [32, 2, 3584, 1024], P('expert', None, None, 'dp'), may hold values from -9 to 9
- first_down: bfloat16 [32, 1024, 3584], P('expert', 'dp'), may hold values from -9 to 9
- second_gate_up: bfloat16 [32, 2, 3584, 1024], P('expert', None, None, 'dp'), may hold values from 1 to 100
- second_down: bfloat16 [32, 1024, 3584], P('expert', 'dp'), may hold values from 1 to 100
Outputs:
- step_gate_up: bfloat16 [32, 2, 3584, 1024], P('expert', None, None, 'dp')
- step_down: bfloat16 [32, 1024, 3584], P('expert', 'dp')
The draws below stay inside these ranges and needn't reach their ends.
Inputs may be any that keep to these rules, and one draw needn't show every extreme that they name: `expert_ids`: among the routes of the rows of one device, no expert is named more than 12 times, and in every draw some device names some expert exactly 12 times. `slot_expert`: each expert once. `swap_flag`: entry k equals entry (k + 16) mod 32; entry 31 is always 1.
All inputs are finite; a program needn't handle non-finite values.
Results may differ from the reference program's by a relative error of at most 0.0087.
Values may be sent and summed in bfloat16 or wider, within the bound.
No kernel may reach another device: no remote copies, remote signals or barrier semaphores. Data moves between devices by JAX's collectives and lax.ppermute only.
A program may use at most 192 MiB of HBM per device.

```python
import math
import jax
import jax.numpy as jnp
import numpy as np
from jax import lax

D = 3584
HID = 1024
TOP = 2
TOK_DEV = 128
EXPERTS = 32
CAP = 12
TOKENS = 16384


def draw_swap_flag(key, part):
    half_count = EXPERTS // 2
    half_flags = jax.random.randint(key, (half_count,), 0, 2).astype(jnp.int32)
    last_mark = (jnp.arange(half_count, dtype=jnp.int32) == half_count - 1).astype(jnp.int32)
    half_flags = jnp.maximum(half_flags, last_mark)
    return jnp.concatenate([half_flags, half_flags])


def level_of(own_key, dims, pieces, low, high):
    def one(axis_at, shards_of):
        steps = jax.random.uniform(jax.random.fold_in(jax.random.fold_in(own_key, 6), axis_at), (shards_of,), jnp.float32, low / len(pieces), high / len(pieces))
        return jnp.repeat(jnp.exp(steps), dims[axis_at] // shards_of).reshape((-1,) + (1,) * (len(dims) - axis_at - 1))

    loudness = one(*pieces[0])
    for cut in pieces[1:]:
        loudness = loudness * one(*cut)
    return loudness


def assign_block(own_key, own, number, rows, number_of, top, limit, skew):
    ranking = jax.random.permutation(own_key, number_of)
    heavy_load, ordinary = shares(number_of, rows * top, limit, skew, True), shares(number_of, rows * top, limit, skew, False)
    places = jnp.arange(number_of)

    def named(sizes, rotation):
        used = int((sizes > 0).sum())
        fixed = max(1, used // 4)
        shifted = fixed + (places - fixed + rotation * (used - fixed)) % max(1, number_of - fixed)
        return jnp.zeros((number_of,), jnp.int32).at[ranking[jnp.where(places < fixed, places, shifted)]].set(jnp.asarray(sizes, jnp.int32))

    sizes = jnp.where(number % 4 == 0, named(heavy_load, number // 4), named(ordinary, number - number // 4 - 1))
    mixed = jax.random.permutation(jax.random.fold_in(own, 3), number_of)
    giver, receiver = mixed[0:number_of // 2 * 2:2], mixed[1:number_of // 2 * 2:2]
    margin = jnp.minimum(sizes[giver] - 1, limit - sizes[receiver]) // 2
    margin = jnp.where((giver == ranking[0]) | (receiver == ranking[0]) | (sizes[receiver] == 0), 0, jnp.maximum(margin, 0))
    shifted = jax.random.randint(jax.random.fold_in(own, 4), (number_of // 2,), 0, 1 << 20) % (margin + 1)
    sizes = sizes.at[giver].add(-shifted).at[receiver].add(shifted)
    members = jnp.searchsorted(jnp.cumsum(sizes), jnp.arange(rows * top), side="right").astype(jnp.int32)
    table = members.reshape(top, rows).T
    table = table[jax.random.permutation(jax.random.fold_in(own, 1), rows)]
    rotation = jax.random.randint(jax.random.fold_in(own, 2), (rows, 1), 0, top)
    return jnp.take_along_axis(table, (jnp.arange(top)[None, :] + rotation) % top, axis=1)


def shares(amount, total, bound, slope, full):
    portions = [(1 << 20) // math.isqrt(standing ** slope) + 1 for standing in range(1, amount + 1)]
    largest = bound if full else min(bound, max(-(-total // amount), total * portions[0] // sum(portions)))
    least = 1 if total - largest >= amount - 1 else 0
    given, rest = [largest] + [least] * (amount - 1), total - largest - least * (amount - 1)
    while rest > 0:
        free = [i for i in range(1, amount) if given[i] < largest] or [i for i in range(1, amount) if given[i] < bound]
        pool, budget = sum([portions[i] for i in free]), rest
        for i in free:
            addition = min(bound - given[i], max(1, budget * portions[i] // pool), rest)
            given[i] = given[i] + addition
            rest = rest - addition
    return np.array(given)


def noise(rng, dims, scale, limit, pieces=(), kind=jnp.bfloat16):
    values = jax.random.normal(rng, dims, jnp.float32) * scale
    if len(pieces) > 0:
        values = level_of(rng, dims, pieces, -0.22, 0.18) * values
    return jnp.clip(values, min=-limit, max=limit).astype(kind)


def setup_inputs(seed: int = 0) -> dict:
    key_list = jax.random.split(jax.random.key(seed), 13)
    tokens = noise(key_list[0], (TOKENS, D), 1.0, 6.0, ((0, 128),))
    cotangent = noise(key_list[1], (TOKENS, D), 1.0, 6.0, ((0, 128),))
    expert_ids_keys = jax.random.split(jax.random.fold_in(key_list[2], 1), TOKENS // TOK_DEV)
    expert_ids_turns = jax.random.permutation(jax.random.fold_in(key_list[2], 3), TOKENS // TOK_DEV)
    expert_ids = jax.vmap(lambda own, number: assign_block(jax.random.fold_in(key_list[2], 2), own, number, TOK_DEV, EXPERTS, TOP, CAP, 2))(expert_ids_keys, expert_ids_turns).reshape((TOKENS, TOP))
    combine = jnp.clip(0.2 + 0.8 * jax.random.uniform(key_list[3], (TOKENS, TOP), jnp.float32) ** level_of(key_list[3], (TOKENS, TOP), ((0, 128),), -0.2, 0.2), 0.2, 1.0)
    slot_expert = jax.random.permutation(key_list[4], EXPERTS).astype(jnp.int32)
    swap_flag = draw_swap_flag(jax.random.fold_in(key_list[12], 71), 0)
    w_gate_up = noise(key_list[6], (EXPERTS, 2, D, HID), D ** -0.5, 0.09375, ((0, 32), (3, 4)))
    w_down = noise(key_list[7], (EXPERTS, HID, D), HID ** -0.5, 0.1875, ((0, 32), (1, 4)))
    first_gate_up = noise(key_list[8], (EXPERTS, 2, D, HID), 1.5, 9.0, ((0, 32), (3, 4)))
    first_down = noise(key_list[9], (EXPERTS, HID, D), 1.5, 9.0, ((0, 32), (1, 4)))
    second_gate_up = jnp.clip(jnp.exp(math.log(100.0) - 4.6051702 * jax.random.uniform(key_list[10], (EXPERTS, 2, D, HID), jnp.float32) ** level_of(key_list[10], (EXPERTS, 2, D, HID), ((0, 32), (3, 4)), -0.2, 0.2)), 1.0, 100.0).astype(jnp.bfloat16)
    second_down = jnp.clip(jnp.exp(math.log(100.0) - 4.6051702 * jax.random.uniform(key_list[11], (EXPERTS, HID, D), jnp.float32) ** level_of(key_list[11], (EXPERTS, HID, D), ((0, 32), (1, 4)), -0.2, 0.2)), 1.0, 100.0).astype(jnp.bfloat16)
    return dict(tokens=tokens, cotangent=cotangent, expert_ids=expert_ids, combine=combine, slot_expert=slot_expert, swap_flag=swap_flag, w_gate_up=w_gate_up, w_down=w_down, first_gate_up=first_gate_up, first_down=first_down, second_gate_up=second_gate_up, second_down=second_down)


def slot_owner(slot_expert, swap_flag):
    experts = slot_expert.shape[0]
    slot_ids = jnp.arange(experts, dtype=jnp.int32)
    moved_expert = jnp.where(swap_flag == 1, jnp.roll(slot_expert, -(experts // 2)), slot_expert)
    owner_slot = lax.optimization_barrier(jnp.sum(jnp.where(moved_expert[:, None] == slot_ids[None, :], slot_ids[:, None], 0), axis=0))
    return owner_slot.astype(jnp.int32)

def adam_step(gradient, first_moment, second_moment):
    first_new = 0.9 * first_moment.astype(jnp.float32) + 0.1 * gradient
    second_new = 0.95 * second_moment.astype(jnp.float32) + 0.05 * gradient * gradient
    return (first_new / (jnp.sqrt(second_new) + 1e-08)).astype(jnp.bfloat16)

def contract_rows(left, right):
    return lax.dot_general(left, right, (((0,), (0,)), ((), ())), preferred_element_type=jnp.float32)

def expert_step(rows, grads_in, gate_up, down, gate_up_first, down_first, gate_up_second, down_second):
    gate_pre = jnp.dot(rows, gate_up[0], preferred_element_type=jnp.float32)
    up_pre = jnp.dot(rows, gate_up[1], preferred_element_type=jnp.float32)
    sigmoid_gate = jax.nn.sigmoid(gate_pre)
    silu_gate = gate_pre * sigmoid_gate
    hidden = (silu_gate * up_pre).astype(jnp.bfloat16)
    down_grad = contract_rows(hidden, grads_in)
    hidden_grad = lax.dot_general(grads_in, down, (((1,), (1,)), ((), ())), preferred_element_type=jnp.float32)
    gate_back = (hidden_grad * up_pre * sigmoid_gate * (1.0 + gate_pre * (1.0 - sigmoid_gate))).astype(jnp.bfloat16)
    up_back = (hidden_grad * silu_gate).astype(jnp.bfloat16)
    gate_up_grad = jnp.stack([contract_rows(rows, gate_back), contract_rows(rows, up_back)])
    return (adam_step(gate_up_grad, gate_up_first, gate_up_second), adam_step(down_grad, down_first, down_second))

def reference(tokens, cotangent, expert_ids, combine, slot_expert, swap_flag, w_gate_up, w_down, first_gate_up, first_down, second_gate_up, second_down):
    experts = slot_expert.shape[0]
    top_count = expert_ids.shape[1]
    sources = tokens.shape[0] // TOK_DEV
    per_source = TOK_DEV * top_count
    slot_ids = jnp.arange(experts, dtype=jnp.int32)
    owner_slot = slot_owner(slot_expert, swap_flag)
    expert_hits = expert_ids[:, :, None] == slot_ids[None, None, :]
    route_slot = lax.optimization_barrier(jnp.sum(jnp.where(expert_hits, owner_slot[None, None, :], 0), axis=2)).astype(jnp.int32)
    route_slot = route_slot.reshape(sources, per_source)
    slot_hits = (route_slot[:, :, None] == slot_ids[None, None, :]).astype(jnp.int32)
    position = (lax.optimization_barrier(jnp.sum(jnp.cumsum(slot_hits, axis=1) * slot_hits, axis=2)) - 1).astype(jnp.int32)
    source_ids = jnp.arange(sources, dtype=jnp.int32)[:, None]
    column = source_ids * CAP + position
    route_ids = source_ids * per_source + jnp.arange(per_source, dtype=jnp.int32)[None, :]
    slot_table = jnp.full((experts, sources * CAP), -1, jnp.int32).at[route_slot, column].set(route_ids)
    combine_flat = combine.reshape(-1)
    half_width = experts // 2

    def one_slot(entry):
        slot_now, entries = entry
        filled = (entries >= 0)[:, None]
        clipped = jnp.maximum(entries, 0)
        token_row = clipped // top_count
        rows = jnp.where(filled, tokens[token_row], jnp.zeros((), tokens.dtype))
        scaled = cotangent[token_row].astype(jnp.float32) * combine_flat[clipped][:, None]
        grads_in = jnp.where(filled, scaled, 0.0).astype(jnp.bfloat16)
        source_slot = jnp.where(swap_flag[slot_now] == 1, (slot_now + half_width) % experts, slot_now)
        return expert_step(rows, grads_in, w_gate_up[source_slot], w_down[source_slot], first_gate_up[source_slot], first_down[source_slot], second_gate_up[source_slot], second_down[source_slot])
    step_gate_up, step_down = lax.map(one_slot, (slot_ids, slot_table))
    return (step_gate_up, step_down)
```

```python
import functools

import jax
import jax.numpy as jnp
from jax import lax
from jax.experimental import pallas as pl
from jax.experimental.pallas import tpu as pltpu
from jax.sharding import PartitionSpec as P

INTERPRET = False
AXES = ("dp", "expert")
YZ = 16
CAP = 12
PAIR = 2 * CAP
F32 = jnp.float32
BF16 = jnp.bfloat16
VMEM_LIMIT = 48 * 1024 * 1024


def device_id(xl, c, yz, xh):
    return ((xl * 2 + c) * YZ + yz) * 2 + xh


def send(value, target):
    pairs = []
    for xl in range(2):
        for c in range(2):
            for yz in range(YZ):
                for xh in range(2):
                    goal = target(xl, c, yz, xh)
                    if goal is not None:
                        pairs.append((device_id(xl, c, yz, xh), device_id(*goal)))
    return lax.ppermute(value, AXES, pairs)


def to_core(xl, c, yz, xh):
    return (xl, 1 - c, yz, xh)


def to_swap(xl, c, yz, xh):
    return (xl, c, yz ^ (YZ // 2), xh)


def token_1(xl, c, yz, xh):
    return None if c == xh else (1 - xl, 1 - c, yz, 1 - xh)


def token_2(xl, c, yz, xh):
    return (1 - xl, c, yz, 1 - xh) if c == xh else (xl, 1 - c, yz, xh)


def token_3(xl, c, yz, xh):
    return (1 - xl, c, yz, xh) if c == xh else (xl, 1 - c, yz, 1 - xh)


def token_4(xl, c, yz, xh):
    return (xl, c, yz, 1 - xh) if c == xh else (1 - xl, 1 - c, yz, xh)


def grad_12(xl, c, yz, xh):
    return (1 - xl, c, yz, xh) if c == xh else (1 - xl, 1 - c, yz, 1 - xh)


def grad_3(xl, c, yz, xh):
    return None if c == xh else (xl, 1 - c, yz, 1 - xh)


def over_yz(value):
    groups = [[yz * 2 + xh for yz in range(YZ)] for xh in range(2)]
    return lax.all_to_all(value, "expert", 0, 0, axis_index_groups=groups, tiled=True)


def params(count=1):
    return pltpu.CompilerParams(
        dimension_semantics=("arbitrary",) * count, vmem_limit_bytes=VMEM_LIMIT
    )


def cost(flops, size):
    return pl.CostEstimate(flops=int(flops), bytes_accessed=int(size), transcendentals=0)


def row_select(side, slots_ref, small_refs):
    rows = YZ * PAIR
    tokens = small_refs[0].shape[1]
    row = lax.broadcasted_iota(jnp.int32, (rows, 1), 0).astype(F32)
    twelve = jnp.floor((row + 0.5) * (1.0 / CAP))
    place = row - twelve * CAP
    dest = jnp.floor((twelve + 0.5) * 0.5)
    block = twelve - dest * 2
    slots = slots_ref[...].astype(F32)
    lane = lax.broadcasted_iota(jnp.int32, (rows, slots.shape[1]), 1).astype(F32)
    named = jnp.sum(
        jnp.where(lane == dest * 2 + side.astype(F32), slots, 0.0), axis=1, keepdims=True
    )
    before = lax.broadcasted_iota(jnp.int32, (tokens, tokens), 0)
    after = lax.broadcasted_iota(jnp.int32, (tokens, tokens), 1)
    earlier = jnp.where(before < after, 1.0, 0.0).astype(BF16)
    picks, weight = [], jnp.zeros((rows, 1), F32)
    for b, small in enumerate(small_refs):
        first = small[0:1, :] == named
        second = small[1:2, :] == named
        hit = jnp.where(first, 1.0, jnp.where(second, 1.0, 0.0))
        position = jnp.dot(hit.astype(BF16), earlier, preferred_element_type=F32)
        wanted = jnp.where(block == float(b), place, -1.0)
        pick = jnp.where(position == wanted, hit, 0.0)
        share = jnp.where(first, small[2:3, :], small[3:4, :])
        weight = weight + jnp.sum(pick * share, axis=1, keepdims=True)
        picks.append(pick.astype(BF16))
    return picks, weight


def grads_kernel(side, slots, small_a, small_b, data_a, data_b, out, picks, weights):
    @pl.when(pl.program_id(0) == 0)
    def _():
        found, weight = row_select(side[0], slots, (small_a, small_b))
        picks[0] = found[0]
        picks[1] = found[1]
        weights[...] = weight

    rows = jnp.dot(picks[0], data_a[...], preferred_element_type=F32)
    rows = rows + jnp.dot(picks[1], data_b[...], preferred_element_type=F32)
    rows = (rows * weights[...]).astype(BF16)
    for yz in range(YZ):
        out[yz] = rows[yz * PAIR : (yz + 1) * PAIR]


def tokens_kernel(
    side, slots, sa, sb, sc, sd, own, data_a, data_b, data_c, data_d, out, picks
):
    @pl.when(pl.program_id(0) == 0)
    def _():
        for group, smalls in enumerate(((sa, sb), (sc, sd))):
            found, _ = row_select(side[0], slots, smalls)
            picks[2 * group] = found[0]
            picks[2 * group + 1] = found[1]

    first = jnp.where(side[1] == 1, own[...], data_a[...])
    for group, (left, right) in enumerate(
        ((first, data_b[...]), (data_c[...], data_d[...]))
    ):
        rows = jnp.dot(picks[2 * group], left, preferred_element_type=F32)
        rows = rows + jnp.dot(picks[2 * group + 1], right, preferred_element_type=F32)
        rows = rows.astype(BF16)
        for yz in range(YZ):
            out[yz, group * PAIR : (group + 1) * PAIR] = rows[yz * PAIR : (yz + 1) * PAIR]


def gather_call(kernel, side, slots, smalls, data, groups, extra):
    count, width = data[0].shape
    step = width // 4
    whole = lambda shape: pl.BlockSpec(shape, lambda j: (0,) * len(shape))
    rows = YZ * PAIR
    return pl.pallas_call(
        kernel,
        grid=(width // step,),
        in_specs=[pl.BlockSpec(memory_space=pltpu.SMEM), whole(slots.shape)]
        + [whole(s.shape) for s in smalls]
        + [pl.BlockSpec((count, step), lambda j: (0, j)) for _ in data],
        out_specs=pl.BlockSpec((YZ, groups * PAIR, step), lambda j: (0, 0, j)),
        out_shape=jax.ShapeDtypeStruct((YZ, groups * PAIR, width), BF16),
        scratch_shapes=[pltpu.VMEM((2 * groups, rows, count), BF16)] + extra,
        compiler_params=params(),
        cost_estimate=cost(
            4 * groups * rows * count * width, 2 * width * (len(data) * count + groups * rows)
        ),
        interpret=INTERPRET,
    )(side, slots, *smalls, *data)


def forward_kernel(rows, grads, gate_up, down, hidden_t, gate_back, up_back, total):
    k = pl.program_id(0)

    @pl.when(k == 0)
    def _():
        total[...] = jnp.zeros_like(total)

    total[0] += jnp.dot(rows[...], gate_up[0, 0], preferred_element_type=F32)
    total[1] += jnp.dot(rows[...], gate_up[0, 1], preferred_element_type=F32)
    total[2] += lax.dot_general(
        grads[...], down[0], (((1,), (1,)), ((), ())), preferred_element_type=F32
    )

    @pl.when(k == pl.num_programs(0) - 1)
    def _():
        gate, up, hidden_grad = total[0], total[1], total[2]
        sigmoid = jax.nn.sigmoid(gate)
        silu = gate * sigmoid
        hidden_t[...] = jnp.transpose(silu * up).astype(BF16)
        gate_back[...] = (
            hidden_grad * up * sigmoid * (1.0 + gate * (1.0 - sigmoid))
        ).astype(BF16)
        up_back[...] = (hidden_grad * silu).astype(BF16)


def forward_call(rows, grads, gate_up, down):
    count, width = rows.shape
    units = down.shape[1]
    step = width // 7
    return pl.pallas_call(
        forward_kernel,
        grid=(width // step,),
        in_specs=[
            pl.BlockSpec((count, step), lambda k: (0, k)),
            pl.BlockSpec((count, step), lambda k: (0, k)),
            pl.BlockSpec((1, 2, step, units), lambda k: (0, 0, k, 0)),
            pl.BlockSpec((1, units, step), lambda k: (0, 0, k)),
        ],
        out_specs=[
            pl.BlockSpec((units, count), lambda k: (0, 0)),
            pl.BlockSpec((count, units), lambda k: (0, 0)),
            pl.BlockSpec((count, units), lambda k: (0, 0)),
        ],
        out_shape=[
            jax.ShapeDtypeStruct((units, count), BF16),
            jax.ShapeDtypeStruct((count, units), BF16),
            jax.ShapeDtypeStruct((count, units), BF16),
        ],
        scratch_shapes=[pltpu.VMEM((3, count, units), F32)],
        compiler_params=params(),
        cost_estimate=cost(
            6 * count * width * units, 2 * width * (2 * count + 3 * units)
        ),
        interpret=INTERPRET,
    )(rows, grads, gate_up, down)


def adam(gradient, first, second):
    first_new = 0.9 * first.astype(F32) + 0.1 * gradient
    second_new = 0.95 * second.astype(F32) + 0.05 * gradient * gradient
    return (first_new / (jnp.sqrt(second_new) + 1e-08)).astype(BF16)


def down_kernel(hidden_a, hidden_b, grads_a, grads_b, first, second, out):
    gradient = jnp.dot(hidden_a[...], grads_a[...], preferred_element_type=F32)
    gradient = gradient + jnp.dot(hidden_b[...], grads_b[...], preferred_element_type=F32)
    out[0] = adam(gradient, first[0], second[0])


def down_call(hiddens, grads, first, second, start, units, step):
    count, width = grads[0].shape
    inner = first.shape[1]
    part = pl.BlockSpec((count, step), lambda j: (0, start + j))
    moment = pl.BlockSpec((1, inner, step), lambda j: (0, 0, start + j))
    whole = pl.BlockSpec((inner, count), lambda j: (0, 0))
    return pl.pallas_call(
        down_kernel,
        grid=(units,),
        in_specs=[whole, whole, part, part, moment, moment],
        out_specs=pl.BlockSpec((1, inner, step), lambda j: (0, 0, j)),
        out_shape=jax.ShapeDtypeStruct((1, inner, units * step), BF16),
        compiler_params=params(),
        cost_estimate=cost(
            4 * count * inner * units * step, 2 * units * step * (2 * count + 3 * inner)
        ),
        interpret=INTERPRET,
    )(*hiddens, *grads, first, second)


def contract_rows(left, right):
    return lax.dot_general(left, right, (((0,), (0,)), ((), ())), preferred_element_type=F32)


def gate_up_kernel(
    rows_a, rows_b, gate_a, up_a, gate_b, up_b, first, second, out
):
    for half, (back_a, back_b) in enumerate(((gate_a, gate_b), (up_a, up_b))):
        gradient = contract_rows(rows_a[...], back_a[...])
        gradient = gradient + contract_rows(rows_b[...], back_b[...])
        out[0, half] = adam(gradient, first[0, half], second[0, half])


def gate_up_call(rows, backs, first, second, start, units, step):
    count, width = rows[0].shape
    inner = first.shape[3]
    part = pl.BlockSpec((count, step), lambda j: (0, start + j))
    moment = pl.BlockSpec((1, 2, step, inner), lambda j: (0, 0, start + j, 0))
    whole = pl.BlockSpec((count, inner), lambda j: (0, 0))
    return pl.pallas_call(
        gate_up_kernel,
        grid=(units,),
        in_specs=[part, part, whole, whole, whole, whole, moment, moment],
        out_specs=pl.BlockSpec((1, 2, step, inner), lambda j: (0, 0, j, 0)),
        out_shape=jax.ShapeDtypeStruct((1, 2, units * step, inner), BF16),
        compiler_params=params(),
        cost_estimate=cost(
            8 * count * inner * units * step, 2 * units * step * (2 * count + 6 * inner)
        ),
        interpret=INTERPRET,
    )(*rows, *backs, first, second)


def place_kernel(swapping, mine, theirs, *rest):
    out = rest[-1]

    @pl.when(swapping[0] == 1)
    def _():
        out[...] = theirs[...]

    @pl.when(swapping[0] != 1)
    def _():
        out[...] = mine[...]


def place(swapping, mine, theirs, whole, shape, start, units, axis):
    block = tuple(
        mine.shape[axis] // units if k == axis else n for k, n in enumerate(mine.shape)
    )
    at = lambda base: lambda j: tuple(base + j if k == axis else 0 for k in range(len(block)))
    old = [] if whole is None else [whole]
    return pl.pallas_call(
        place_kernel,
        grid=(units,),
        in_specs=[
            pl.BlockSpec(memory_space=pltpu.SMEM),
            pl.BlockSpec(block, at(0)),
            pl.BlockSpec(block, at(0)),
        ]
        + [pl.BlockSpec(memory_space=pl.ANY) for _ in old],
        out_specs=pl.BlockSpec(block, at(start)),
        out_shape=jax.ShapeDtypeStruct(shape, BF16),
        input_output_aliases={3: 0} if old else {},
        compiler_params=params(),
        cost_estimate=cost(0, 6 * mine.size),
        interpret=INTERPRET,
    )(swapping, mine, theirs, *old)


def local(
    tokens,
    cotangent,
    expert_ids,
    combine,
    slot_expert,
    swap_flag,
    w_gate_up,
    w_down,
    first_gate_up,
    first_down,
    second_gate_up,
    second_down,
):
    width = tokens.shape[1]
    core = lax.axis_index("dp") % 2
    my_slot = lax.axis_index("expert")
    side = my_slot % 2
    near = (core == side).astype(jnp.int32)
    slots = slot_expert[None, :]
    small = jnp.concatenate([expert_ids.T.astype(F32), combine.T], axis=0)

    small_core = send(small, to_core)
    cotangent_core = send(cotangent, to_core)
    tokens_in = [send(tokens, t) for t in (token_1, token_2, token_3, token_4)]
    scaled = gather_call(
        grads_kernel,
        jnp.stack([core, near]).astype(jnp.int32),
        slots,
        [small, small_core],
        [cotangent, cotangent_core],
        1,
        [pltpu.VMEM((YZ * PAIR, 1), F32)],
    )
    small_in = [send(small, t) for t in (token_1, token_2, token_3, token_4)]
    small_in[0] = jnp.where(near == 1, small, small_in[0])
    grads_0 = over_yz(scaled)

    sent_rows = gather_call(
        tokens_kernel,
        jnp.stack([side, near]).astype(jnp.int32),
        slots,
        small_in,
        [tokens] + tokens_in,
        2,
        [],
    )
    grads_12 = send(grads_0, grad_12)
    grads_3 = send(grads_0, grad_3)
    rows_a = over_yz(sent_rows).reshape(-1, width)
    grads_a = jnp.concatenate(
        [
            jnp.where(near == 1, grads_0, grads_12),
            jnp.where(near == 1, grads_12, grads_3),
        ],
        axis=1,
    ).reshape(-1, width)
    grads_b = send(grads_a, to_core)
    rows_b = send(rows_a, to_core)

    hidden_a, gate_a, up_a = forward_call(rows_a, grads_a, w_gate_up, w_down)
    hidden_b, gate_b, up_b = forward_call(rows_b, grads_b, w_gate_up, w_down)

    swapping = swap_flag[my_slot].reshape(1)
    step = width // 7
    step_down = step_gate_up = None
    pending, start = [], 0
    for units in (1, 3, 3):
        mine = down_call(
            (hidden_a, hidden_b), (grads_a, grads_b), first_down, second_down, start, units, step
        )
        pending.append((0, mine, send(mine, to_swap), start, units))
        start += units
    start = 0
    for units in (2, 2, 2, 1):
        mine = gate_up_call(
            (rows_a, rows_b),
            (gate_a, up_a, gate_b, up_b),
            first_gate_up,
            second_gate_up,
            start,
            units,
            step,
        )
        pending.append((1, mine, send(mine, to_swap), start, units))
        start += units
    for kind, mine, theirs, start, units in pending:
        if kind == 0:
            step_down = place(
                swapping, mine, theirs, step_down, w_down.shape, start, units, 2
            )
        else:
            step_gate_up = place(
                swapping, mine, theirs, step_gate_up, w_gate_up.shape, start, units, 2
            )
    return (step_gate_up, step_down)


def solution(mesh):
    return jax.shard_map(
        local,
        mesh=mesh,
        in_specs=(
            P(("dp", "expert"), None),
            P(("dp", "expert"), None),
            P(("dp", "expert"), None),
            P(("dp", "expert"), None),
            P(),
            P(),
            P("expert", None, None, "dp"),
            P("expert", "dp", None),
            P("expert", None, None, "dp"),
            P("expert", "dp", None),
            P("expert", None, None, "dp"),
            P("expert", "dp", None),
        ),
        out_specs=(P("expert", None, None, "dp"), P("expert", "dp", None)),
        check_vma=False,
    )
```

```python
import jax
import jax.numpy as jnp
from jax import lax
from jax.experimental import pallas as pl
from jax.experimental.pallas import tpu as pltpu
from jax.sharding import PartitionSpec as P


INTERPRET = False
AXES = ("dp", "expert")
YZ = 16
CAP = 12
PAIR = 2 * CAP
F32 = jnp.float32
BF16 = jnp.bfloat16


def device_id(xl, c, yz, xh):
    return ((xl * 2 + c) * YZ + yz) * 2 + xh


def send(value, target):
    pairs = []
    for xl in range(2):
        for c in range(2):
            for yz in range(YZ):
                for xh in range(2):
                    goal = target(xl, c, yz, xh)
                    if goal is not None:
                        pairs.append((device_id(xl, c, yz, xh), device_id(*goal)))
    return lax.ppermute(value, AXES, pairs)


def to_core(xl, c, yz, xh):
    return (xl, 1 - c, yz, xh)


def to_swap(xl, c, yz, xh):
    return (xl, c, yz ^ (YZ // 2), xh)


def token_1(xl, c, yz, xh):
    return None if c == xh else (1 - xl, 1 - c, yz, 1 - xh)


def token_2(xl, c, yz, xh):
    return (1 - xl, c, yz, 1 - xh) if c == xh else (xl, 1 - c, yz, xh)


def token_3(xl, c, yz, xh):
    return (1 - xl, c, yz, xh) if c == xh else (xl, 1 - c, yz, 1 - xh)


def token_4(xl, c, yz, xh):
    return (xl, c, yz, 1 - xh) if c == xh else (1 - xl, 1 - c, yz, xh)


def grad_12(xl, c, yz, xh):
    return (1 - xl, c, yz, xh) if c == xh else (1 - xl, 1 - c, yz, 1 - xh)


def grad_3(xl, c, yz, xh):
    return None if c == xh else (xl, 1 - c, yz, 1 - xh)


def over_yz(value):
    groups = [[yz * 2 + xh for yz in range(YZ)] for xh in range(2)]
    return lax.all_to_all(value, "expert", 0, 0, axis_index_groups=groups, tiled=True)


def params(count=1):
    return pltpu.CompilerParams(
        dimension_semantics=("arbitrary",) * count
    )


def cost(flops, size):
    return pl.CostEstimate(flops=int(flops), bytes_accessed=int(size), transcendentals=0)


def row_select(side, slots_ref, small_refs):
    rows = YZ * PAIR
    tokens = small_refs[0].shape[1]
    row = lax.broadcasted_iota(jnp.int32, (rows, 1), 0).astype(F32)
    twelve = jnp.floor((row + 0.5) * (1.0 / CAP))
    place = row - twelve * CAP
    dest = jnp.floor((twelve + 0.5) * 0.5)
    block = twelve - dest * 2
    slots = slots_ref[...].astype(F32)
    lane = lax.broadcasted_iota(jnp.int32, (rows, slots.shape[1]), 1).astype(F32)
    named = jnp.sum(
        jnp.where(lane == dest * 2 + side.astype(F32), slots, 0.0), axis=1, keepdims=True
    )
    before = lax.broadcasted_iota(jnp.int32, (tokens, tokens), 0)
    after = lax.broadcasted_iota(jnp.int32, (tokens, tokens), 1)
    earlier = jnp.where(before < after, 1.0, 0.0).astype(BF16)
    picks, weight = [], jnp.zeros((rows, 1), F32)
    for b, small in enumerate(small_refs):
        first = small[0:1, :] == named
        second = small[1:2, :] == named
        hit = jnp.where(first, 1.0, jnp.where(second, 1.0, 0.0))
        position = jnp.dot(hit.astype(BF16), earlier, preferred_element_type=F32)
        wanted = jnp.where(block == float(b), place, -1.0)
        pick = jnp.where(position == wanted, hit, 0.0)
        share = jnp.where(first, small[2:3, :], small[3:4, :])
        weight = weight + jnp.sum(pick * share, axis=1, keepdims=True)
        picks.append(pick.astype(BF16))
    return picks, weight


def grads_kernel(side, slots, small_a, small_b, data_a, data_b, out, picks, weights):
    @pl.when(pl.program_id(0) == 0)
    def _():
        found, weight = row_select(side[0], slots, (small_a, small_b))
        picks[0] = found[0]
        picks[1] = found[1]
        weights[...] = weight

    rows = jnp.dot(picks[0], data_a[...], preferred_element_type=F32)
    rows = rows + jnp.dot(picks[1], data_b[...], preferred_element_type=F32)
    rows = (rows * weights[...]).astype(BF16)
    for yz in range(YZ):
        out[yz] = rows[yz * PAIR : (yz + 1) * PAIR]


def tokens_kernel(
    side, slots, sa, sb, sc, sd, own, data_a, data_b, data_c, data_d, out, picks
):
    @pl.when(pl.program_id(0) == 0)
    def _():
        for group, smalls in enumerate(((sa, sb), (sc, sd))):
            found, _ = row_select(side[0], slots, smalls)
            picks[2 * group] = found[0]
            picks[2 * group + 1] = found[1]

    first = jnp.where(side[1] == 1, own[...], data_a[...])
    for group, (left, right) in enumerate(
        ((first, data_b[...]), (data_c[...], data_d[...]))
    ):
        rows = jnp.dot(picks[2 * group], left, preferred_element_type=F32)
        rows = rows + jnp.dot(picks[2 * group + 1], right, preferred_element_type=F32)
        rows = rows.astype(BF16)
        for yz in range(YZ):
            out[yz, group * PAIR : (group + 1) * PAIR] = rows[yz * PAIR : (yz + 1) * PAIR]


def gather_call(kernel, side, slots, smalls, data, groups, extra):
    count, width = data[0].shape
    step = width // 4
    whole = lambda shape: pl.BlockSpec(shape, lambda j: (0,) * len(shape))
    rows = YZ * PAIR
    return pl.pallas_call(
        kernel,
        grid=(width // step,),
        in_specs=[pl.BlockSpec(memory_space=pltpu.SMEM), whole(slots.shape)]
        + [whole(s.shape) for s in smalls]
        + [pl.BlockSpec((count, step), lambda j: (0, j)) for _ in data],
        out_specs=pl.BlockSpec((YZ, groups * PAIR, step), lambda j: (0, 0, j)),
        out_shape=jax.ShapeDtypeStruct((YZ, groups * PAIR, width), BF16),
        scratch_shapes=[pltpu.VMEM((2 * groups, rows, count), BF16)] + extra,
        compiler_params=params(),
        cost_estimate=cost(
            4 * groups * rows * count * width, 2 * width * (len(data) * count + groups * rows)
        ),
        interpret=INTERPRET,
    )(side, slots, *smalls, *data)


def hidden_grad_kernel(grads, down_a, down_b, out):
    @pl.when(pl.program_id(0) == 0)
    def _():
        out[...] = jnp.zeros_like(out)

    for k, down in enumerate((down_a, down_b)):
        out[k] += lax.dot_general(
            grads[...], down[0], (((1,), (1,)), ((), ())), preferred_element_type=F32
        )


def hidden_grad_call(grads, down_a, down_b):
    count, width = grads.shape
    units = down_a.shape[1]
    step = width // 7
    weight = pl.BlockSpec((1, units, step), lambda k: (0, 0, k))
    return pl.pallas_call(
        hidden_grad_kernel,
        grid=(width // step,),
        in_specs=[pl.BlockSpec((count, step), lambda k: (0, k)), weight, weight],
        out_specs=pl.BlockSpec((2, count, units), lambda k: (0, 0, 0)),
        out_shape=jax.ShapeDtypeStruct((2, count, units), F32),
        compiler_params=params(),
        cost_estimate=cost(
            4 * count * width * units, 2 * width * (count + 2 * units) + 8 * count * units
        ),
        interpret=INTERPRET,
    )(grads, down_a, down_b)


def forward_kernel(
    rows, gate_up_a, gate_up_b, hidden_grads, hidden_a, hidden_b, back_a, back_b, total
):
    k = pl.program_id(0)

    @pl.when(k == 0)
    def _():
        total[...] = jnp.zeros_like(total)

    for owner, gate_up in enumerate((gate_up_a, gate_up_b)):
        for half in range(2):
            total[2 * owner + half] += jnp.dot(
                rows[...], gate_up[0, half], preferred_element_type=F32
            )

    @pl.when(k == pl.num_programs(0) - 1)
    def _():
        units = hidden_a.shape[0]
        for owner, (hidden_t, back) in enumerate(((hidden_a, back_a), (hidden_b, back_b))):
            gate, up, hidden_grad = total[2 * owner], total[2 * owner + 1], hidden_grads[owner]
            sigmoid = jax.nn.sigmoid(gate)
            silu = gate * sigmoid
            hidden_t[...] = jnp.transpose(silu * up).astype(BF16)
            back[:, :units] = (
                hidden_grad * up * sigmoid * (1.0 + gate * (1.0 - sigmoid))
            ).astype(BF16)
            back[:, units:] = (hidden_grad * silu).astype(BF16)


def forward_call(rows, gate_up_a, gate_up_b, hidden_grads):
    count, width = rows.shape
    units = gate_up_a.shape[3]
    step = width // 7
    weight = pl.BlockSpec((1, 2, step, units), lambda k: (0, 0, k, 0))
    whole = lambda shape: pl.BlockSpec(shape, lambda k: (0,) * len(shape))
    shapes = [(units, count), (units, count), (count, 2 * units), (count, 2 * units)]
    return pl.pallas_call(
        forward_kernel,
        grid=(width // step,),
        in_specs=[
            pl.BlockSpec((count, step), lambda k: (0, k)),
            weight,
            weight,
            whole(hidden_grads.shape),
        ],
        out_specs=[whole(s) for s in shapes],
        out_shape=[jax.ShapeDtypeStruct(s, BF16) for s in shapes],
        scratch_shapes=[pltpu.VMEM((4, count, units), F32)],
        compiler_params=params(),
        cost_estimate=cost(8 * count * width * units, 2 * width * (count + 4 * units)),
        interpret=INTERPRET,
    )(rows, gate_up_a, gate_up_b, hidden_grads)


def adam(gradient, first, second):
    first_new = 0.9 * first.astype(F32) + 0.1 * gradient
    second_new = 0.95 * second.astype(F32) + 0.05 * gradient * gradient
    return (first_new / (jnp.sqrt(second_new) + 1e-08)).astype(BF16)


def after(kernel, count):
    return lambda *refs: kernel(*refs[count:])


def down_kernel(hidden_a, hidden_b, grads_a, grads_b, first, second, out):
    gradient = jnp.dot(hidden_a[...], grads_a[...], preferred_element_type=F32)
    gradient = gradient + jnp.dot(hidden_b[...], grads_b[...], preferred_element_type=F32)
    out[0] = adam(gradient, first[0], second[0])


def down_call(behind, hiddens, grads, first, second, start, units, step):
    count, _ = grads[0].shape
    inner = first.shape[1]
    part = pl.BlockSpec((count, step), lambda j: (0, start + j))
    moment = pl.BlockSpec((1, inner, step), lambda j: (0, 0, start + j))
    whole = pl.BlockSpec((inner, count), lambda j: (0, 0))
    return pl.pallas_call(
        after(down_kernel, len(behind)),
        grid=(units,),
        in_specs=[pl.BlockSpec(memory_space=pl.ANY) for _ in behind]
        + [whole, whole, part, part, moment, moment],
        out_specs=pl.BlockSpec((1, inner, step), lambda j: (0, 0, j)),
        out_shape=jax.ShapeDtypeStruct((1, inner, units * step), BF16),
        compiler_params=params(),
        cost_estimate=cost(
            4 * count * inner * units * step, 2 * units * step * (2 * count + 3 * inner)
        ),
        interpret=INTERPRET,
    )(*behind, *hiddens, *grads, first, second)


def contract_rows(left, right):
    return lax.dot_general(left, right, (((0,), (0,)), ((), ())), preferred_element_type=F32)


def gate_up_kernel(rows_a, rows_b, back_a, back_b, first, second, out):
    inner = first.shape[3]
    gradient = contract_rows(rows_a[...], back_a[...])
    gradient = gradient + contract_rows(rows_b[...], back_b[...])
    for half in range(2):
        out[0, half] = adam(
            gradient[:, half * inner : (half + 1) * inner], first[0, half], second[0, half]
        )


def gate_up_call(behind, rows, backs, first, second, start, units, step):
    count, _ = rows[0].shape
    inner = first.shape[3]
    part = pl.BlockSpec((count, step), lambda j: (0, start + j))
    moment = pl.BlockSpec((1, 2, step, inner), lambda j: (0, 0, start + j, 0))
    whole = pl.BlockSpec((count, 2 * inner), lambda j: (0, 0))
    return pl.pallas_call(
        after(gate_up_kernel, len(behind)),
        grid=(units,),
        in_specs=[pl.BlockSpec(memory_space=pl.ANY) for _ in behind]
        + [part, part, whole, whole, moment, moment],
        out_specs=pl.BlockSpec((1, 2, step, inner), lambda j: (0, 0, j, 0)),
        out_shape=jax.ShapeDtypeStruct((1, 2, units * step, inner), BF16),
        compiler_params=params(),
        cost_estimate=cost(
            8 * count * inner * units * step, 2 * units * step * (2 * count + 6 * inner)
        ),
        interpret=INTERPRET,
    )(*behind, *rows, *backs, first, second)


def place_kernel(swapping, mine, theirs, *rest):
    out = rest[-1]

    @pl.when(swapping[0] == 1)
    def _():
        out[...] = theirs[...]

    @pl.when(swapping[0] != 1)
    def _():
        out[...] = mine[...]


def place(behind, swapping, mine, theirs, whole, shape, start, units):
    block = tuple(n // units if k == 2 else n for k, n in enumerate(mine.shape))
    at = lambda base: lambda j: tuple(base + j if k == 2 else 0 for k in range(len(block)))
    old = behind + ([] if whole is None else [whole])
    return pl.pallas_call(
        place_kernel,
        grid=(units,),
        in_specs=[
            pl.BlockSpec(memory_space=pltpu.SMEM),
            pl.BlockSpec(block, at(0)),
            pl.BlockSpec(block, at(0)),
        ]
        + [pl.BlockSpec(memory_space=pl.ANY) for _ in old],
        out_specs=pl.BlockSpec(block, at(start)),
        out_shape=jax.ShapeDtypeStruct(shape, BF16),
        input_output_aliases={} if whole is None else {2 + len(old): 0},
        compiler_params=params(),
        cost_estimate=cost(0, 6 * mine.size),
        interpret=INTERPRET,
    )(swapping, mine, theirs, *old)


def local(
    tokens,
    cotangent,
    expert_ids,
    combine,
    slot_expert,
    swap_flag,
    w_gate_up,
    w_down,
    first_gate_up,
    first_down,
    second_gate_up,
    second_down,
):
    width = tokens.shape[1]
    core = lax.axis_index("dp") % 2
    my_slot = lax.axis_index("expert")
    side = my_slot % 2
    near = (core == side).astype(jnp.int32)
    slots = slot_expert[None, :]
    small = jnp.concatenate([expert_ids.T.astype(F32), combine.T], axis=0)
    token_goals = (token_1, token_2, token_3, token_4)

    small_core = send(small, to_core)
    cotangent_core = send(cotangent, to_core)
    small_in = [send(small, t) for t in token_goals]
    tokens_in = [send(tokens, t) for t in token_goals]
    scaled = gather_call(
        grads_kernel,
        jnp.stack([core, near]).astype(jnp.int32),
        slots,
        [small, small_core],
        [cotangent, cotangent_core],
        1,
        [pltpu.VMEM((YZ * PAIR, 1), F32)],
    )
    small_in[0] = jnp.where(near == 1, small, small_in[0])
    grads_0 = over_yz(scaled)
    down_core = send(w_down, to_core)
    gate_up_core = send(w_gate_up, to_core)

    sent_rows = gather_call(
        tokens_kernel,
        jnp.stack([side, near]).astype(jnp.int32),
        slots,
        small_in,
        [tokens] + tokens_in,
        2,
        [],
    )
    grads_12 = send(grads_0, grad_12)
    grads_3 = send(grads_0, grad_3)
    rows_a = over_yz(sent_rows).reshape(-1, width)
    grads_a = jnp.concatenate(
        [
            jnp.where(near == 1, grads_0, grads_12),
            jnp.where(near == 1, grads_12, grads_3),
        ],
        axis=1,
    ).reshape(-1, width)
    grads_b = send(grads_a, to_core)
    hidden_grads = hidden_grad_call(grads_a, w_down, down_core)

    hidden_a, hidden_other, back_a, back_other = forward_call(
        rows_a, w_gate_up, gate_up_core, hidden_grads
    )
    hidden_b = send(hidden_other, to_core)
    back_b = send(back_other, to_core)
    rows_b = send(rows_a, to_core)

    swapping = swap_flag[my_slot].reshape(1)
    pending, behind, start, step = [], [], 0, width // 7
    for units in (1, 3, 3):
        mine = down_call(
            behind,
            (hidden_a, hidden_b),
            (grads_a, grads_b),
            first_down,
            second_down,
            start,
            units,
            step,
        )
        theirs = send(mine, to_swap)
        pending.append((mine, theirs, start, units))
        behind, start = [mine], start + units
    downs = len(pending)
    start, step = 0, width // 14
    for units in (4, 4, 4, 1, 1):
        mine = gate_up_call(
            behind,
            (rows_a, rows_b),
            (back_a, back_b),
            first_gate_up,
            second_gate_up,
            start,
            units,
            step,
        )
        theirs = send(mine, to_swap)
        pending.append((mine, theirs, start, units))
        behind, start = [mine], start + units
    whole = None
    for mine, theirs, start, units in pending[:downs]:
        whole = place([], swapping, mine, theirs, whole, w_down.shape, start, units)
    step_down, whole, behind = whole, None, [whole]
    for mine, theirs, start, units in pending[downs:]:
        whole = place(behind, swapping, mine, theirs, whole, w_gate_up.shape, start, units)
        behind = []
    return (whole, step_down)


def solution(mesh):
    return jax.shard_map(
        local,
        mesh=mesh,
        in_specs=(
            P(("dp", "expert"), None),
            P(("dp", "expert"), None),
            P(("dp", "expert"), None),
            P(("dp", "expert"), None),
            P(),
            P(),
            P("expert", None, None, "dp"),
            P("expert", "dp", None),
            P("expert", None, None, "dp"),
            P("expert", "dp", None),
            P("expert", None, None, "dp"),
            P("expert", "dp", None),
        ),
        out_specs=(P("expert", None, None, "dp"), P("expert", "dp", None)),
        check_vma=False,
    )
```

```python
import jax
import jax.numpy as jnp
from jax import lax
from jax.experimental import pallas as pl
from jax.experimental.pallas import tpu as pltpu
from jax.sharding import PartitionSpec as P


INTERPRET = False
AXES = ("dp", "expert")
YZ = 16
CAP = 12
PAIR = 2 * CAP
GATHER_STEPS = 4
FORWARD_STEPS = 4
F32 = jnp.float32
BF16 = jnp.bfloat16


def device_id(xl, c, yz, xh):
    return ((xl * 2 + c) * YZ + yz) * 2 + xh


def send(value, target):
    pairs = []
    for xl in range(2):
        for c in range(2):
            for yz in range(YZ):
                for xh in range(2):
                    goal = target(xl, c, yz, xh)
                    if goal is not None:
                        pairs.append((device_id(xl, c, yz, xh), device_id(*goal)))
    return lax.ppermute(value, AXES, pairs)


def to_core(xl, c, yz, xh):
    return (xl, 1 - c, yz, xh)


def to_swap(xl, c, yz, xh):
    return (xl, c, yz ^ (YZ // 2), xh)


def token_1(xl, c, yz, xh):
    return None if c == xh else (1 - xl, 1 - c, yz, 1 - xh)


def token_2(xl, c, yz, xh):
    return (1 - xl, c, yz, 1 - xh) if c == xh else (xl, 1 - c, yz, xh)


def token_3(xl, c, yz, xh):
    return (1 - xl, c, yz, xh) if c == xh else (xl, 1 - c, yz, 1 - xh)


def token_4(xl, c, yz, xh):
    return (xl, c, yz, 1 - xh) if c == xh else (1 - xl, 1 - c, yz, xh)


def grad_12(xl, c, yz, xh):
    return (1 - xl, c, yz, xh) if c == xh else (1 - xl, 1 - c, yz, 1 - xh)


def grad_3(xl, c, yz, xh):
    return None if c == xh else (xl, 1 - c, yz, 1 - xh)


def over_yz(value):
    groups = [[yz * 2 + xh for yz in range(YZ)] for xh in range(2)]
    return lax.all_to_all(value, "expert", 0, 0, axis_index_groups=groups, tiled=True)


def params(count=1):
    return pltpu.CompilerParams(
        dimension_semantics=("arbitrary",) * count
    )


def cost(flops, size):
    return pl.CostEstimate(flops=int(flops), bytes_accessed=int(size), transcendentals=0)


def row_select(side, slots_ref, small_refs):
    rows = YZ * PAIR
    tokens = small_refs[0].shape[1]
    row = lax.broadcasted_iota(jnp.int32, (rows, 1), 0).astype(F32)
    twelve = jnp.floor((row + 0.5) * (1.0 / CAP))
    place = row - twelve * CAP
    dest = jnp.floor((twelve + 0.5) * 0.5)
    block = twelve - dest * 2
    slots = slots_ref[...].astype(F32)
    lane = lax.broadcasted_iota(jnp.int32, (rows, slots.shape[1]), 1).astype(F32)
    named = jnp.sum(
        jnp.where(lane == dest * 2 + side.astype(F32), slots, 0.0), axis=1, keepdims=True
    )
    before = lax.broadcasted_iota(jnp.int32, (tokens, tokens), 0)
    after = lax.broadcasted_iota(jnp.int32, (tokens, tokens), 1)
    earlier = jnp.where(before < after, 1.0, 0.0).astype(BF16)
    picks, weight = [], jnp.zeros((rows, 1), F32)
    for b, small in enumerate(small_refs):
        first = small[0:1, :] == named
        second = small[1:2, :] == named
        hit = jnp.where(first, 1.0, jnp.where(second, 1.0, 0.0))
        position = jnp.dot(hit.astype(BF16), earlier, preferred_element_type=F32)
        wanted = jnp.where(block == float(b), place, -1.0)
        pick = jnp.where(position == wanted, hit, 0.0)
        share = jnp.where(first, small[2:3, :], small[3:4, :])
        weight = weight + jnp.sum(pick * share, axis=1, keepdims=True)
        picks.append(pick.astype(BF16))
    return picks, weight


def picks_kernel(side, slots, *refs):
    out = refs[-1]
    tokens = refs[0].shape[1]
    for group in range(out.shape[0]):
        found, _ = row_select(side[0], slots, refs[2 * group : 2 * group + 2])
        out[group, :, :tokens] = found[0]
        out[group, :, tokens:] = found[1]


def picks_call(side, slots, smalls):
    return pl.pallas_call(
        picks_kernel,
        in_specs=[pl.BlockSpec(memory_space=pltpu.SMEM)]
        + [pl.BlockSpec(memory_space=pltpu.VMEM)] * (1 + len(smalls)),
        out_specs=pl.BlockSpec(memory_space=pltpu.VMEM),
        out_shape=jax.ShapeDtypeStruct(
            (len(smalls) // 2, YZ * PAIR, 2 * smalls[0].shape[1]), BF16
        ),
        cost_estimate=cost(10**8, 10**6),
        interpret=INTERPRET,
    )(side, slots, *smalls)


def grads_kernel(side, slots, small_a, small_b, data_a, data_b, out, picks, weights, both):
    count = data_a.shape[0]

    @pl.when(pl.program_id(0) == 0)
    def _():
        found, weight = row_select(side[0], slots, (small_a, small_b))
        picks[:, :count] = found[0]
        picks[:, count:] = found[1]
        weights[...] = weight

    both[:count] = data_a[...]
    both[count:] = data_b[...]
    rows = jnp.dot(picks[...], both[...], preferred_element_type=F32)
    rows = (rows * weights[...]).astype(BF16)
    for yz in range(YZ):
        out[yz] = rows[yz * PAIR : (yz + 1) * PAIR]


def grads_call(side, slots, smalls, data):
    count, width = data[0].shape
    step = width // GATHER_STEPS
    whole = lambda shape: pl.BlockSpec(shape, lambda j: (0,) * len(shape))
    rows = YZ * PAIR
    return pl.pallas_call(
        grads_kernel,
        grid=(width // step,),
        in_specs=[pl.BlockSpec(memory_space=pltpu.SMEM), whole(slots.shape)]
        + [whole(s.shape) for s in smalls]
        + [pl.BlockSpec((count, step), lambda j: (0, j)) for _ in data],
        out_specs=pl.BlockSpec((YZ, PAIR, step), lambda j: (0, 0, j)),
        out_shape=jax.ShapeDtypeStruct((YZ, PAIR, width), BF16),
        scratch_shapes=[
            pltpu.VMEM((rows, 2 * count), BF16),
            pltpu.VMEM((rows, 1), F32),
            pltpu.VMEM((2 * count, step), BF16),
        ],
        compiler_params=params(),
        cost_estimate=cost(4 * rows * count * width, 2 * width * (2 * count + rows)),
        interpret=INTERPRET,
    )(side, slots, *smalls, *data)


def tokens_kernel(near, picks, own, data_a, data_b, data_c, data_d, out, both):
    count = own.shape[0]

    @pl.when(near[0] == 1)
    def _():
        both[:count] = own[...]

    @pl.when(near[0] != 1)
    def _():
        both[:count] = data_a[...]

    both[count : 2 * count] = data_b[...]
    both[2 * count : 3 * count] = data_c[...]
    both[3 * count :] = data_d[...]
    for group in range(2):
        rows = jnp.dot(
            picks[group],
            both[2 * group * count : 2 * (group + 1) * count],
            preferred_element_type=F32,
        ).astype(BF16)
        for yz in range(YZ):
            out[yz, group * PAIR : (group + 1) * PAIR] = rows[yz * PAIR : (yz + 1) * PAIR]


def tokens_call(near, picks, data):
    count, width = data[0].shape
    step = width // GATHER_STEPS
    rows = YZ * PAIR
    return pl.pallas_call(
        tokens_kernel,
        grid=(width // step,),
        in_specs=[
            pl.BlockSpec(memory_space=pltpu.SMEM),
            pl.BlockSpec(picks.shape, lambda j: (0, 0, 0)),
        ]
        + [pl.BlockSpec((count, step), lambda j: (0, j)) for _ in data],
        out_specs=pl.BlockSpec((YZ, 2 * PAIR, step), lambda j: (0, 0, j)),
        out_shape=jax.ShapeDtypeStruct((YZ, 2 * PAIR, width), BF16),
        scratch_shapes=[pltpu.VMEM((4 * count, step), BF16)],
        compiler_params=params(),
        cost_estimate=cost(8 * rows * count * width, 2 * width * (5 * count + 2 * rows)),
        interpret=INTERPRET,
    )(near, picks, *data)


def marker_kernel(near, rows, out):
    out[0] = near[0]


def marker_call(near, rows):
    return pl.pallas_call(
        marker_kernel,
        in_specs=[
            pl.BlockSpec(memory_space=pltpu.SMEM),
            pl.BlockSpec(memory_space=pl.ANY),
        ],
        out_specs=pl.BlockSpec(memory_space=pltpu.SMEM),
        out_shape=jax.ShapeDtypeStruct((1,), jnp.int32),
        interpret=INTERPRET,
    )(near, rows)


def hidden_grad_kernel(near, own, near_in, far_in, down_a, down_b, rows, out):
    @pl.when(pl.program_id(0) == 0)
    def _():
        out[...] = jnp.zeros_like(out)

    @pl.when(near[0] == 1)
    def _():
        rows[:, :PAIR] = own[...]
        rows[:, PAIR:] = near_in[...]

    @pl.when(near[0] != 1)
    def _():
        rows[:, :PAIR] = near_in[...]
        rows[:, PAIR:] = far_in[...]

    grads = rows[...].reshape(-1, rows.shape[2])
    for k, down in enumerate((down_a, down_b)):
        out[k] += lax.dot_general(
            grads, down[0], (((1,), (1,)), ((), ())), preferred_element_type=F32
        )


def hidden_grad_call(near, pieces, down_a, down_b):
    width = pieces[0].shape[2]
    units = down_a.shape[1]
    count = 2 * YZ * PAIR
    step = width // FORWARD_STEPS
    weight = pl.BlockSpec((1, units, step), lambda k: (0, 0, k))
    return pl.pallas_call(
        hidden_grad_kernel,
        grid=(width // step,),
        in_specs=[pl.BlockSpec(memory_space=pltpu.SMEM)]
        + [pl.BlockSpec((YZ, PAIR, step), lambda k: (0, 0, k)) for _ in pieces]
        + [weight, weight],
        out_specs=[
            pl.BlockSpec((YZ, 2 * PAIR, step), lambda k: (0, 0, k)),
            pl.BlockSpec((2, count, units), lambda k: (0, 0, 0)),
        ],
        out_shape=[
            jax.ShapeDtypeStruct((YZ, 2 * PAIR, width), BF16),
            jax.ShapeDtypeStruct((2, count, units), F32),
        ],
        compiler_params=params(),
        cost_estimate=cost(
            4 * count * width * units, 5 * width * count + 4 * width * units + 8 * count * units
        ),
        interpret=INTERPRET,
    )(near, *pieces, down_a, down_b)


def forward_kernel(
    rows, gate_up_a, gate_up_b, hidden_grads, hidden_a, hidden_b, back_a, back_b, total
):
    k = pl.program_id(0)

    @pl.when(k == 0)
    def _():
        total[...] = jnp.zeros_like(total)

    for owner, gate_up in enumerate((gate_up_a, gate_up_b)):
        for half in range(2):
            total[2 * owner + half] += jnp.dot(
                rows[...], gate_up[0, half], preferred_element_type=F32
            )

    @pl.when(k == pl.num_programs(0) - 1)
    def _():
        units = hidden_a.shape[0]
        for owner, (hidden_t, back) in enumerate(((hidden_a, back_a), (hidden_b, back_b))):
            gate, up, hidden_grad = total[2 * owner], total[2 * owner + 1], hidden_grads[owner]
            sigmoid = jax.nn.sigmoid(gate)
            silu = gate * sigmoid
            hidden_t[...] = jnp.transpose(silu * up).astype(BF16)
            back[:, :units] = (
                hidden_grad * up * sigmoid * (1.0 + gate * (1.0 - sigmoid))
            ).astype(BF16)
            back[:, units:] = (hidden_grad * silu).astype(BF16)


def forward_call(rows, gate_up_a, gate_up_b, hidden_grads):
    count, width = rows.shape
    units = gate_up_a.shape[3]
    step = width // FORWARD_STEPS
    weight = pl.BlockSpec((1, 2, step, units), lambda k: (0, 0, k, 0))
    whole = lambda shape: pl.BlockSpec(shape, lambda k: (0,) * len(shape))
    shapes = [(units, count), (units, count), (count, 2 * units), (count, 2 * units)]
    return pl.pallas_call(
        forward_kernel,
        grid=(width // step,),
        in_specs=[
            pl.BlockSpec((count, step), lambda k: (0, k)),
            weight,
            weight,
            whole(hidden_grads.shape),
        ],
        out_specs=[whole(s) for s in shapes],
        out_shape=[jax.ShapeDtypeStruct(s, BF16) for s in shapes],
        scratch_shapes=[pltpu.VMEM((4, count, units), F32)],
        compiler_params=params(),
        cost_estimate=cost(8 * count * width * units, 2 * width * (count + 4 * units)),
        interpret=INTERPRET,
    )(rows, gate_up_a, gate_up_b, hidden_grads)


def adam(gradient, first, second):
    first_new = 0.9 * first.astype(F32) + 0.1 * gradient
    second_new = 0.95 * second.astype(F32) + 0.05 * gradient * gradient
    return (first_new / (jnp.sqrt(second_new) + 1e-08)).astype(BF16)


def after(kernel, count):
    return lambda *refs: kernel(*refs[count:])


def down_kernel(hidden_a, hidden_b, grads_a, grads_b, first, second, out):
    gradient = jnp.dot(hidden_a[...], grads_a[...], preferred_element_type=F32)
    gradient = gradient + jnp.dot(hidden_b[...], grads_b[...], preferred_element_type=F32)
    out[0] = adam(gradient, first[0], second[0])


def down_call(behind, hiddens, grads, first, second, start, units, step):
    count, _ = grads[0].shape
    inner = first.shape[1]
    part = pl.BlockSpec((count, step), lambda j: (0, start + j))
    moment = pl.BlockSpec((1, inner, step), lambda j: (0, 0, start + j))
    whole = pl.BlockSpec((inner, count), lambda j: (0, 0))
    return pl.pallas_call(
        after(down_kernel, len(behind)),
        grid=(units,),
        in_specs=[pl.BlockSpec(memory_space=pl.ANY) for _ in behind]
        + [whole, whole, part, part, moment, moment],
        out_specs=pl.BlockSpec((1, inner, step), lambda j: (0, 0, j)),
        out_shape=jax.ShapeDtypeStruct((1, inner, units * step), BF16),
        compiler_params=params(),
        cost_estimate=cost(
            4 * count * inner * units * step, 2 * units * step * (2 * count + 3 * inner)
        ),
        interpret=INTERPRET,
    )(*behind, *hiddens, *grads, first, second)


def contract_rows(left, right):
    return lax.dot_general(left, right, (((0,), (0,)), ((), ())), preferred_element_type=F32)


def gate_up_kernel(rows_a, rows_b, back_a, back_b, first, second, out):
    inner = first.shape[3]
    gradient = contract_rows(rows_a[...], back_a[...])
    gradient = gradient + contract_rows(rows_b[...], back_b[...])
    for half in range(2):
        out[0, half] = adam(
            gradient[:, half * inner : (half + 1) * inner], first[0, half], second[0, half]
        )


def gate_up_call(behind, rows, backs, first, second, start, units, step):
    count, _ = rows[0].shape
    inner = first.shape[3]
    part = pl.BlockSpec((count, step), lambda j: (0, start + j))
    moment = pl.BlockSpec((1, 2, step, inner), lambda j: (0, 0, start + j, 0))
    whole = pl.BlockSpec((count, 2 * inner), lambda j: (0, 0))
    return pl.pallas_call(
        after(gate_up_kernel, len(behind)),
        grid=(units,),
        in_specs=[pl.BlockSpec(memory_space=pl.ANY) for _ in behind]
        + [part, part, whole, whole, moment, moment],
        out_specs=pl.BlockSpec((1, 2, step, inner), lambda j: (0, 0, j, 0)),
        out_shape=jax.ShapeDtypeStruct((1, 2, units * step, inner), BF16),
        compiler_params=params(),
        cost_estimate=cost(
            8 * count * inner * units * step, 2 * units * step * (2 * count + 6 * inner)
        ),
        interpret=INTERPRET,
    )(*behind, *rows, *backs, first, second)


def place_kernel(swapping, mine, theirs, *rest):
    out = rest[-1]

    @pl.when(swapping[0] == 1)
    def _():
        out[...] = theirs[...]

    @pl.when(swapping[0] != 1)
    def _():
        out[...] = mine[...]


def place(behind, swapping, mine, theirs, whole, shape, start, units):
    block = tuple(n // units if k == 2 else n for k, n in enumerate(mine.shape))
    at = lambda base: lambda j: tuple(base + j if k == 2 else 0 for k in range(len(block)))
    old = behind + ([] if whole is None else [whole])
    return pl.pallas_call(
        place_kernel,
        grid=(units,),
        in_specs=[
            pl.BlockSpec(memory_space=pltpu.SMEM),
            pl.BlockSpec(block, at(0)),
            pl.BlockSpec(block, at(0)),
        ]
        + [pl.BlockSpec(memory_space=pl.ANY) for _ in old],
        out_specs=pl.BlockSpec(block, at(start)),
        out_shape=jax.ShapeDtypeStruct(shape, BF16),
        input_output_aliases={} if whole is None else {2 + len(old): 0},
        compiler_params=params(),
        cost_estimate=cost(0, 6 * mine.size),
        interpret=INTERPRET,
    )(swapping, mine, theirs, *old)


def local(
    tokens,
    cotangent,
    expert_ids,
    combine,
    slot_expert,
    swap_flag,
    w_gate_up,
    w_down,
    first_gate_up,
    first_down,
    second_gate_up,
    second_down,
):
    width = tokens.shape[1]
    core = lax.axis_index("dp") % 2
    my_slot = lax.axis_index("expert")
    side = my_slot % 2
    near = (core == side).astype(jnp.int32)
    slots = slot_expert[None, :]
    small = jnp.concatenate([expert_ids.T.astype(F32), combine.T], axis=0)
    token_goals = (token_1, token_2, token_3, token_4)

    small_core = send(small, to_core)
    cotangent_core = send(cotangent, to_core)
    small_in = [send(small, t) for t in token_goals]
    tokens_in = [send(tokens, t) for t in token_goals]
    near = near.reshape(1)
    scaled = grads_call(
        core.astype(jnp.int32).reshape(1), slots, [small, small_core], [cotangent, cotangent_core]
    )
    small_in[0] = jnp.where(near == 1, small, small_in[0])
    grads_0 = over_yz(scaled)
    down_core = send(w_down, to_core)
    gate_up_core = send(w_gate_up, to_core)

    picks = picks_call(side.astype(jnp.int32).reshape(1), slots, small_in)
    sent_rows = tokens_call(near, picks, [tokens] + tokens_in)
    grads_12 = send(grads_0, grad_12)
    grads_3 = send(grads_0, grad_3)
    rows_a = over_yz(sent_rows).reshape(-1, width)
    near = marker_call(near, rows_a)
    grads_a, hidden_grads = hidden_grad_call(near, [grads_0, grads_12, grads_3], w_down, down_core)
    grads_a = grads_a.reshape(-1, width)
    grads_b = send(grads_a, to_core)

    hidden_a, hidden_other, back_a, back_other = forward_call(
        rows_a, w_gate_up, gate_up_core, hidden_grads
    )
    hidden_b = send(hidden_other, to_core)
    back_b = send(back_other, to_core)
    rows_b = send(rows_a, to_core)

    swapping = swap_flag[my_slot].reshape(1)
    pending, behind, start, step = [], [], 0, width // 7
    for units in (1, 3, 3):
        mine = down_call(
            behind,
            (hidden_a, hidden_b),
            (grads_a, grads_b),
            first_down,
            second_down,
            start,
            units,
            step,
        )
        theirs = send(mine, to_swap)
        pending.append((mine, theirs, start, units))
        behind, start = [mine], start + units
    downs = len(pending)
    start, step = 0, width // 14
    for units in (4, 4, 4, 1, 1):
        mine = gate_up_call(
            behind,
            (rows_a, rows_b),
            (back_a, back_b),
            first_gate_up,
            second_gate_up,
            start,
            units,
            step,
        )
        theirs = send(mine, to_swap)
        pending.append((mine, theirs, start, units))
        behind, start = [mine], start + units
    whole = None
    for mine, theirs, start, units in pending[:downs]:
        whole = place([], swapping, mine, theirs, whole, w_down.shape, start, units)
    step_down, whole, behind = whole, None, [whole]
    for mine, theirs, start, units in pending[downs:]:
        whole = place(behind, swapping, mine, theirs, whole, w_gate_up.shape, start, units)
        behind = []
    return (whole, step_down)


def solution(mesh):
    return jax.shard_map(
        local,
        mesh=mesh,
        in_specs=(
            P(("dp", "expert"), None),
            P(("dp", "expert"), None),
            P(("dp", "expert"), None),
            P(("dp", "expert"), None),
            P(),
            P(),
            P("expert", None, None, "dp"),
            P("expert", "dp", None),
            P("expert", None, None, "dp"),
            P("expert", "dp", None),
            P("expert", None, None, "dp"),
            P("expert", "dp", None),
        ),
        out_specs=(P("expert", None, None, "dp"), P("expert", "dp", None)),
        check_vma=False,
    )
```

```python
import jax
import jax.numpy as jnp
from jax import lax
from jax.experimental import pallas as pl
from jax.experimental.pallas import tpu as pltpu
from jax.sharding import PartitionSpec as P


INTERPRET = False
AXES = ("dp", "expert")
YZ = 16
CAP = 12
PAIR = 2 * CAP
GATHER_STEPS = 2
FORWARD_STEPS = 4
F32 = jnp.float32
BF16 = jnp.bfloat16


def device_id(xl, c, yz, xh):
    return ((xl * 2 + c) * YZ + yz) * 2 + xh


def send(value, target):
    pairs = []
    for xl in range(2):
        for c in range(2):
            for yz in range(YZ):
                for xh in range(2):
                    goal = target(xl, c, yz, xh)
                    if goal is not None:
                        pairs.append((device_id(xl, c, yz, xh), device_id(*goal)))
    return lax.ppermute(value, AXES, pairs)


def to_core(xl, c, yz, xh):
    return (xl, 1 - c, yz, xh)


def to_swap(xl, c, yz, xh):
    return (xl, c, yz ^ (YZ // 2), xh)


def token_1(xl, c, yz, xh):
    return None if c == xh else (1 - xl, 1 - c, yz, 1 - xh)


def token_2(xl, c, yz, xh):
    return (1 - xl, c, yz, 1 - xh) if c == xh else (xl, 1 - c, yz, xh)


def token_3(xl, c, yz, xh):
    return (1 - xl, c, yz, xh) if c == xh else (xl, 1 - c, yz, 1 - xh)


def token_4(xl, c, yz, xh):
    return (xl, c, yz, 1 - xh) if c == xh else (1 - xl, 1 - c, yz, xh)


def grad_12(xl, c, yz, xh):
    return (1 - xl, c, yz, xh) if c == xh else (1 - xl, 1 - c, yz, 1 - xh)


def grad_3(xl, c, yz, xh):
    return None if c == xh else (xl, 1 - c, yz, 1 - xh)


def over_yz(value):
    groups = [[yz * 2 + xh for yz in range(YZ)] for xh in range(2)]
    return lax.all_to_all(value, "expert", 0, 0, axis_index_groups=groups, tiled=True)


def params(count=1):
    return pltpu.CompilerParams(
        dimension_semantics=("arbitrary",) * count
    )


def cost(flops, size):
    return pl.CostEstimate(flops=int(flops), bytes_accessed=int(size), transcendentals=0)


def row_select(side, slots_ref, small_refs):
    rows = YZ * PAIR
    tokens = small_refs[0].shape[1]
    row = lax.broadcasted_iota(jnp.int32, (rows, 1), 0).astype(F32)
    twelve = jnp.floor((row + 0.5) * (1.0 / CAP))
    place = row - twelve * CAP
    dest = jnp.floor((twelve + 0.5) * 0.5)
    block = twelve - dest * 2
    slots = slots_ref[...].astype(F32)
    lane = lax.broadcasted_iota(jnp.int32, (rows, slots.shape[1]), 1).astype(F32)
    named = jnp.sum(
        jnp.where(lane == dest * 2 + side.astype(F32), slots, 0.0), axis=1, keepdims=True
    )
    before = lax.broadcasted_iota(jnp.int32, (tokens, tokens), 0)
    after = lax.broadcasted_iota(jnp.int32, (tokens, tokens), 1)
    earlier = jnp.where(before < after, 1.0, 0.0).astype(BF16)
    picks, weight = [], jnp.zeros((rows, 1), F32)
    for b, small in enumerate(small_refs):
        first = small[0:1, :] == named
        second = small[1:2, :] == named
        hit = jnp.where(first, 1.0, jnp.where(second, 1.0, 0.0))
        position = jnp.dot(hit.astype(BF16), earlier, preferred_element_type=F32)
        wanted = jnp.where(block == float(b), place, -1.0)
        pick = jnp.where(position == wanted, hit, 0.0)
        share = jnp.where(first, small[2:3, :], small[3:4, :])
        weight = weight + jnp.sum(pick * share, axis=1, keepdims=True)
        picks.append(pick.astype(BF16))
    return picks, weight


def picks_kernel(side, slots, *refs):
    out = refs[-1]
    tokens = refs[0].shape[1]
    for group in range(out.shape[0]):
        found, _ = row_select(side[0], slots, refs[2 * group : 2 * group + 2])
        out[group, :, :tokens] = found[0]
        out[group, :, tokens:] = found[1]


def picks_call(side, slots, smalls):
    return pl.pallas_call(
        picks_kernel,
        in_specs=[pl.BlockSpec(memory_space=pltpu.SMEM)]
        + [pl.BlockSpec(memory_space=pltpu.VMEM)] * (1 + len(smalls)),
        out_specs=pl.BlockSpec(memory_space=pltpu.VMEM),
        out_shape=jax.ShapeDtypeStruct(
            (len(smalls) // 2, YZ * PAIR, 2 * smalls[0].shape[1]), BF16
        ),
        cost_estimate=cost(10**8, 10**6),
        interpret=INTERPRET,
    )(side, slots, *smalls)


def grads_kernel(side, slots, small_a, small_b, data_a, data_b, out, picks, weights, both):
    count = data_a.shape[0]

    @pl.when(pl.program_id(0) == 0)
    def _():
        found, weight = row_select(side[0], slots, (small_a, small_b))
        picks[:, :count] = found[0]
        picks[:, count:] = found[1]
        weights[...] = weight

    both[:count] = data_a[...]
    both[count:] = data_b[...]
    rows = jnp.dot(picks[...], both[...], preferred_element_type=F32)
    rows = (rows * weights[...]).astype(BF16)
    for yz in range(YZ):
        out[yz] = rows[yz * PAIR : (yz + 1) * PAIR]


def grads_call(side, slots, smalls, data):
    count, width = data[0].shape
    step = width // GATHER_STEPS
    whole = lambda shape: pl.BlockSpec(shape, lambda j: (0,) * len(shape))
    rows = YZ * PAIR
    return pl.pallas_call(
        grads_kernel,
        grid=(width // step,),
        in_specs=[pl.BlockSpec(memory_space=pltpu.SMEM), whole(slots.shape)]
        + [whole(s.shape) for s in smalls]
        + [pl.BlockSpec((count, step), lambda j: (0, j)) for _ in data],
        out_specs=pl.BlockSpec((YZ, PAIR, step), lambda j: (0, 0, j)),
        out_shape=jax.ShapeDtypeStruct((YZ, PAIR, width), BF16),
        scratch_shapes=[
            pltpu.VMEM((rows, 2 * count), BF16),
            pltpu.VMEM((rows, 1), F32),
            pltpu.VMEM((2 * count, step), BF16),
        ],
        compiler_params=params(),
        cost_estimate=cost(4 * rows * count * width, 2 * width * (2 * count + rows)),
        interpret=INTERPRET,
    )(side, slots, *smalls, *data)


def tokens_kernel(near, picks, own, data_a, data_b, data_c, data_d, out, both):
    count = own.shape[0]

    @pl.when(near[0] == 1)
    def _():
        both[:count] = own[...]

    @pl.when(near[0] != 1)
    def _():
        both[:count] = data_a[...]

    both[count : 2 * count] = data_b[...]
    both[2 * count : 3 * count] = data_c[...]
    both[3 * count :] = data_d[...]
    for group in range(2):
        rows = jnp.dot(
            picks[group],
            both[2 * group * count : 2 * (group + 1) * count],
            preferred_element_type=F32,
        ).astype(BF16)
        for yz in range(YZ):
            out[yz, group * PAIR : (group + 1) * PAIR] = rows[yz * PAIR : (yz + 1) * PAIR]


def tokens_call(near, picks, data):
    count, width = data[0].shape
    step = width // GATHER_STEPS
    rows = YZ * PAIR
    return pl.pallas_call(
        tokens_kernel,
        grid=(width // step,),
        in_specs=[
            pl.BlockSpec(memory_space=pltpu.SMEM),
            pl.BlockSpec(picks.shape, lambda j: (0, 0, 0)),
        ]
        + [pl.BlockSpec((count, step), lambda j: (0, j)) for _ in data],
        out_specs=pl.BlockSpec((YZ, 2 * PAIR, step), lambda j: (0, 0, j)),
        out_shape=jax.ShapeDtypeStruct((YZ, 2 * PAIR, width), BF16),
        scratch_shapes=[pltpu.VMEM((4 * count, step), BF16)],
        compiler_params=params(),
        cost_estimate=cost(8 * rows * count * width, 2 * width * (5 * count + 2 * rows)),
        interpret=INTERPRET,
    )(near, picks, *data)


def marker_kernel(near, rows, out):
    out[0] = near[0]


def marker_call(near, rows):
    return pl.pallas_call(
        marker_kernel,
        in_specs=[
            pl.BlockSpec(memory_space=pltpu.SMEM),
            pl.BlockSpec(memory_space=pl.ANY),
        ],
        out_specs=pl.BlockSpec(memory_space=pltpu.SMEM),
        out_shape=jax.ShapeDtypeStruct((1,), jnp.int32),
        interpret=INTERPRET,
    )(near, rows)


def forward_kernel(rows, gate_up_a, gate_up_b, hidden_a, hidden_b, total):
    k = pl.program_id(0)

    @pl.when(k == 0)
    def _():
        total[...] = jnp.zeros_like(total)

    for owner, gate_up in enumerate((gate_up_a, gate_up_b)):
        for half in range(2):
            total[2 * owner + half] += jnp.dot(
                rows[...], gate_up[0, half], preferred_element_type=F32
            )

    @pl.when(k == pl.num_programs(0) - 1)
    def _():
        for owner, hidden_t in enumerate((hidden_a, hidden_b)):
            gate, up = total[2 * owner], total[2 * owner + 1]
            hidden_t[...] = jnp.transpose(gate * jax.nn.sigmoid(gate) * up).astype(BF16)


def forward_call(rows, gate_up_a, gate_up_b):
    count, width = rows.shape
    units = gate_up_a.shape[3]
    step = width // FORWARD_STEPS
    weight = pl.BlockSpec((1, 2, step, units), lambda k: (0, 0, k, 0))
    whole = lambda shape: pl.BlockSpec(shape, lambda k: (0,) * len(shape))
    shapes = [((units, count), BF16), ((units, count), BF16), ((4, count, units), F32)]
    return pl.pallas_call(
        forward_kernel,
        grid=(width // step,),
        in_specs=[pl.BlockSpec((count, step), lambda k: (0, k)), weight, weight],
        out_specs=[whole(s) for s, _ in shapes],
        out_shape=[jax.ShapeDtypeStruct(*s) for s in shapes],
        compiler_params=params(),
        cost_estimate=cost(8 * count * width * units, 2 * width * (count + 4 * units)),
        interpret=INTERPRET,
    )(rows, gate_up_a, gate_up_b)


def backward_kernel(grads, down_a, down_b, gates, back_a, back_b, total):
    k = pl.program_id(0)

    @pl.when(k == 0)
    def _():
        total[...] = jnp.zeros_like(total)

    for owner, down in enumerate((down_a, down_b)):
        total[owner] += lax.dot_general(
            grads[...], down[0], (((1,), (1,)), ((), ())), preferred_element_type=F32
        )

    @pl.when(k == pl.num_programs(0) - 1)
    def _():
        units = total.shape[2]
        for owner, back in enumerate((back_a, back_b)):
            gate, up, hidden_grad = gates[2 * owner], gates[2 * owner + 1], total[owner]
            sigmoid = jax.nn.sigmoid(gate)
            back[:, :units] = (
                hidden_grad * up * sigmoid * (1.0 + gate * (1.0 - sigmoid))
            ).astype(BF16)
            back[:, units:] = (hidden_grad * (gate * sigmoid)).astype(BF16)


def backward_call(behind, grads, down_a, down_b, gates):
    count, width = grads.shape
    units = down_a.shape[1]
    step = width // FORWARD_STEPS
    weight = pl.BlockSpec((1, units, step), lambda k: (0, 0, k))
    whole = lambda shape: pl.BlockSpec(shape, lambda k: (0,) * len(shape))
    return pl.pallas_call(
        after(backward_kernel, len(behind)),
        grid=(width // step,),
        in_specs=[pl.BlockSpec(memory_space=pl.ANY) for _ in behind]
        + [
            pl.BlockSpec((count, step), lambda k: (0, k)),
            weight,
            weight,
            whole(gates.shape),
        ],
        out_specs=[whole((count, 2 * units))] * 2,
        out_shape=[jax.ShapeDtypeStruct((count, 2 * units), BF16)] * 2,
        scratch_shapes=[pltpu.VMEM((2, count, units), F32)],
        compiler_params=params(),
        cost_estimate=cost(
            4 * count * width * units, 2 * width * (count + 2 * units) + 16 * count * units
        ),
        interpret=INTERPRET,
    )(*behind, grads, down_a, down_b, gates)


def adam(gradient, first, second):
    first_new = 0.9 * first.astype(F32) + 0.1 * gradient
    second_new = 0.95 * second.astype(F32) + 0.05 * gradient * gradient
    return (first_new / (jnp.sqrt(second_new) + 1e-08)).astype(BF16)


def after(kernel, count):
    return lambda *refs: kernel(*refs[count:])


def down_kernel(hidden_a, hidden_b, grads_a, grads_b, first, second, out):
    gradient = jnp.dot(hidden_a[...], grads_a[...], preferred_element_type=F32)
    gradient = gradient + jnp.dot(hidden_b[...], grads_b[...], preferred_element_type=F32)
    out[0] = adam(gradient, first[0], second[0])


def down_call(behind, hiddens, grads, first, second, start, units, step):
    count, _ = grads[0].shape
    inner = first.shape[1]
    part = pl.BlockSpec((count, step), lambda j: (0, start + j))
    moment = pl.BlockSpec((1, inner, step), lambda j: (0, 0, start + j))
    whole = pl.BlockSpec((inner, count), lambda j: (0, 0))
    return pl.pallas_call(
        after(down_kernel, len(behind)),
        grid=(units,),
        in_specs=[pl.BlockSpec(memory_space=pl.ANY) for _ in behind]
        + [whole, whole, part, part, moment, moment],
        out_specs=pl.BlockSpec((1, inner, step), lambda j: (0, 0, j)),
        out_shape=jax.ShapeDtypeStruct((1, inner, units * step), BF16),
        compiler_params=params(),
        cost_estimate=cost(
            4 * count * inner * units * step, 2 * units * step * (2 * count + 3 * inner)
        ),
        interpret=INTERPRET,
    )(*behind, *hiddens, *grads, first, second)


def contract_rows(left, right):
    return lax.dot_general(left, right, (((0,), (0,)), ((), ())), preferred_element_type=F32)


def gate_up_kernel(rows_a, rows_b, back_a, back_b, first, second, out):
    inner = first.shape[3]
    gradient = contract_rows(rows_a[...], back_a[...])
    gradient = gradient + contract_rows(rows_b[...], back_b[...])
    for half in range(2):
        out[0, half] = adam(
            gradient[:, half * inner : (half + 1) * inner], first[0, half], second[0, half]
        )


def gate_up_call(behind, rows, backs, first, second, start, units, step):
    count, _ = rows[0].shape
    inner = first.shape[3]
    part = pl.BlockSpec((count, step), lambda j: (0, start + j))
    moment = pl.BlockSpec((1, 2, step, inner), lambda j: (0, 0, start + j, 0))
    whole = pl.BlockSpec((count, 2 * inner), lambda j: (0, 0))
    return pl.pallas_call(
        after(gate_up_kernel, len(behind)),
        grid=(units,),
        in_specs=[pl.BlockSpec(memory_space=pl.ANY) for _ in behind]
        + [part, part, whole, whole, moment, moment],
        out_specs=pl.BlockSpec((1, 2, step, inner), lambda j: (0, 0, j, 0)),
        out_shape=jax.ShapeDtypeStruct((1, 2, units * step, inner), BF16),
        compiler_params=params(),
        cost_estimate=cost(
            8 * count * inner * units * step, 2 * units * step * (2 * count + 6 * inner)
        ),
        interpret=INTERPRET,
    )(*behind, *rows, *backs, first, second)


def place_kernel(swapping, mine, theirs, *rest):
    out = rest[-1]

    @pl.when(swapping[0] == 1)
    def _():
        out[...] = theirs[...]

    @pl.when(swapping[0] != 1)
    def _():
        out[...] = mine[...]


def place(behind, swapping, mine, theirs, whole, shape, start, units):
    block = tuple(n // units if k == 2 else n for k, n in enumerate(mine.shape))
    at = lambda base: lambda j: tuple(base + j if k == 2 else 0 for k in range(len(block)))
    old = behind + ([] if whole is None else [whole])
    return pl.pallas_call(
        place_kernel,
        grid=(units,),
        in_specs=[
            pl.BlockSpec(memory_space=pltpu.SMEM),
            pl.BlockSpec(block, at(0)),
            pl.BlockSpec(block, at(0)),
        ]
        + [pl.BlockSpec(memory_space=pl.ANY) for _ in old],
        out_specs=pl.BlockSpec(block, at(start)),
        out_shape=jax.ShapeDtypeStruct(shape, BF16),
        input_output_aliases={} if whole is None else {2 + len(old): 0},
        compiler_params=params(),
        cost_estimate=cost(0, 6 * mine.size),
        interpret=INTERPRET,
    )(swapping, mine, theirs, *old)


def join_grads(near, own, near_in, far_in):
    first = jnp.where(near == 1, own, near_in)
    second = jnp.where(near == 1, near_in, far_in)
    return jnp.concatenate([first, second], axis=1).reshape(-1, own.shape[2])


def local(
    tokens,
    cotangent,
    expert_ids,
    combine,
    slot_expert,
    swap_flag,
    w_gate_up,
    w_down,
    first_gate_up,
    first_down,
    second_gate_up,
    second_down,
):
    width = tokens.shape[1]
    core = lax.axis_index("dp") % 2
    my_slot = lax.axis_index("expert")
    side = my_slot % 2
    near = (core == side).astype(jnp.int32)
    slots = slot_expert[None, :]
    small = jnp.concatenate([expert_ids.T.astype(F32), combine.T], axis=0)
    token_goals = (token_1, token_2, token_3, token_4)

    small_core = send(small, to_core)
    cotangent_core = send(cotangent, to_core)
    small_in = [send(small, t) for t in token_goals]
    tokens_in = [send(tokens, t) for t in token_goals]
    near = near.reshape(1)
    scaled = grads_call(
        core.astype(jnp.int32).reshape(1), slots, [small, small_core], [cotangent, cotangent_core]
    )
    small_in[0] = jnp.where(near == 1, small, small_in[0])
    grads_0 = over_yz(scaled)
    down_core = send(w_down, to_core)
    gate_up_core = send(w_gate_up, to_core)

    picks = picks_call(side.astype(jnp.int32).reshape(1), slots, small_in)
    sent_rows = tokens_call(near, picks, [tokens] + tokens_in)
    grads_12 = send(grads_0, grad_12)
    grads_3 = send(grads_0, grad_3)
    rows_a = over_yz(sent_rows).reshape(-1, width)
    near = marker_call(near, rows_a)
    grads_a = join_grads(near, grads_0, grads_12, grads_3)
    grads_b = send(grads_a, to_core)

    hidden_a, hidden_other, gates = forward_call(rows_a, w_gate_up, gate_up_core)
    hidden_b = send(hidden_other, to_core)
    rows_b = send(rows_a, to_core)

    swapping = swap_flag[my_slot].reshape(1)
    pending, behind, start, step = [], [], 0, width // 7
    for units in (1, 3, 3):
        mine = down_call(
            behind,
            (hidden_a, hidden_b),
            (grads_a, grads_b),
            first_down,
            second_down,
            start,
            units,
            step,
        )
        theirs = send(mine, to_swap)
        pending.append((mine, theirs, start, units))
        behind, start = [mine], start + units
    downs = len(pending)
    back_a, back_other = backward_call(behind, grads_a, w_down, down_core, gates)
    back_b = send(back_other, to_core)
    start, step = 0, width // 14
    for units in (4, 4, 4, 1, 1):
        mine = gate_up_call(
            behind,
            (rows_a, rows_b),
            (back_a, back_b),
            first_gate_up,
            second_gate_up,
            start,
            units,
            step,
        )
        theirs = send(mine, to_swap)
        pending.append((mine, theirs, start, units))
        behind, start = [mine], start + units
    whole = None
    for mine, theirs, start, units in pending[:downs]:
        whole = place([], swapping, mine, theirs, whole, w_down.shape, start, units)
    step_down, whole, behind = whole, None, [whole]
    for mine, theirs, start, units in pending[downs:]:
        whole = place(behind, swapping, mine, theirs, whole, w_gate_up.shape, start, units)
        behind = []
    return (whole, step_down)


def solution(mesh):
    return jax.shard_map(
        local,
        mesh=mesh,
        in_specs=(
            P(("dp", "expert"), None),
            P(("dp", "expert"), None),
            P(("dp", "expert"), None),
            P(("dp", "expert"), None),
            P(),
            P(),
            P("expert", None, None, "dp"),
            P("expert", "dp", None),
            P("expert", None, None, "dp"),
            P("expert", "dp", None),
            P("expert", None, None, "dp"),
            P("expert", "dp", None),
        ),
        out_specs=(P("expert", None, None, "dp"), P("expert", "dp", None)),
        check_vma=False,
    )
```

```python
import jax
import jax.numpy as jnp
from jax import lax
from jax.experimental import pallas as pl
from jax.experimental.pallas import tpu as pltpu
from jax.sharding import PartitionSpec as P


INTERPRET = False
AXES = ("dp", "expert")
YZ = 16
CAP = 12
PAIR = 2 * CAP
GATHER_STEPS = 2
FORWARD_STEPS = 4
F32 = jnp.float32
BF16 = jnp.bfloat16


def device_id(xl, c, yz, xh):
    return ((xl * 2 + c) * YZ + yz) * 2 + xh


def send(value, target):
    pairs = []
    for xl in range(2):
        for c in range(2):
            for yz in range(YZ):
                for xh in range(2):
                    goal = target(xl, c, yz, xh)
                    if goal is not None:
                        pairs.append((device_id(xl, c, yz, xh), device_id(*goal)))
    return lax.ppermute(value, AXES, pairs)


def to_core(xl, c, yz, xh):
    return (xl, 1 - c, yz, xh)


def to_swap(xl, c, yz, xh):
    return (xl, c, yz ^ (YZ // 2), xh)


def token_1(xl, c, yz, xh):
    return None if c == xh else (1 - xl, 1 - c, yz, 1 - xh)


def token_2(xl, c, yz, xh):
    return (1 - xl, c, yz, 1 - xh) if c == xh else (xl, 1 - c, yz, xh)


def token_3(xl, c, yz, xh):
    return (1 - xl, c, yz, xh) if c == xh else (xl, 1 - c, yz, 1 - xh)


def token_4(xl, c, yz, xh):
    return (xl, c, yz, 1 - xh) if c == xh else (1 - xl, 1 - c, yz, xh)


def grad_near(xl, c, yz, xh):
    return (xl, 1 - c, yz, xh) if c == xh else None


def grad_far(xl, c, yz, xh):
    return None if c == xh else (xl, 1 - c, yz, xh)


def small_near(xl, c, yz, xh):
    return None if c == xh else (1 - xl, 1 - c, yz, 1 - xh)


def grad_12(xl, c, yz, xh):
    return (1 - xl, c, yz, xh) if c == xh else (1 - xl, 1 - c, yz, 1 - xh)


def grad_3(xl, c, yz, xh):
    return None if c == xh else (xl, 1 - c, yz, 1 - xh)


def over_yz(value):
    groups = [[yz * 2 + xh for yz in range(YZ)] for xh in range(2)]
    return lax.all_to_all(value, "expert", 0, 0, axis_index_groups=groups, tiled=True)


def params(count=1):
    return pltpu.CompilerParams(
        dimension_semantics=("arbitrary",) * count
    )


def cost(flops, size):
    return pl.CostEstimate(flops=int(flops), bytes_accessed=int(size), transcendentals=0)


def row_select(side, slots_ref, small_refs):
    rows = YZ * PAIR
    tokens = small_refs[0].shape[1]
    row = lax.broadcasted_iota(jnp.int32, (rows, 1), 0).astype(F32)
    twelve = jnp.floor((row + 0.5) * (1.0 / CAP))
    place = row - twelve * CAP
    dest = jnp.floor((twelve + 0.5) * 0.5)
    block = twelve - dest * 2
    slots = slots_ref[...].astype(F32)
    lane = lax.broadcasted_iota(jnp.int32, (rows, slots.shape[1]), 1).astype(F32)
    named = jnp.sum(
        jnp.where(lane == dest * 2 + side.astype(F32), slots, 0.0), axis=1, keepdims=True
    )
    before = lax.broadcasted_iota(jnp.int32, (tokens, tokens), 0)
    after = lax.broadcasted_iota(jnp.int32, (tokens, tokens), 1)
    earlier = jnp.where(before < after, 1.0, 0.0).astype(BF16)
    picks, weight = [], jnp.zeros((rows, 1), F32)
    for b, small in enumerate(small_refs):
        first = small[0:1, :] == named
        second = small[1:2, :] == named
        hit = jnp.where(first, 1.0, jnp.where(second, 1.0, 0.0))
        position = jnp.dot(hit.astype(BF16), earlier, preferred_element_type=F32)
        wanted = jnp.where(block == float(b), place, -1.0)
        pick = jnp.where(position == wanted, hit, 0.0)
        share = jnp.where(first, small[2:3, :], small[3:4, :])
        weight = weight + jnp.sum(pick * share, axis=1, keepdims=True)
        picks.append(pick.astype(BF16))
    return picks, weight


def picks_kernel(side, slots, near_small, far_small, out):
    tokens = near_small.shape[1]
    for group, small in enumerate((near_small[...], far_small[...])):
        half = small.shape[0] // 2
        found, _ = row_select(side[0], slots, (small[:half], small[half:]))
        out[group, :, :tokens] = found[0]
        out[group, :, tokens:] = found[1]


def picks_call(side, slots, near_small, far_small):
    return pl.pallas_call(
        picks_kernel,
        in_specs=[pl.BlockSpec(memory_space=pltpu.SMEM)]
        + [pl.BlockSpec(memory_space=pltpu.VMEM)] * 3,
        out_specs=pl.BlockSpec(memory_space=pltpu.VMEM),
        out_shape=jax.ShapeDtypeStruct((2, YZ * PAIR, 2 * near_small.shape[1]), BF16),
        cost_estimate=cost(10**8, 10**6),
        interpret=INTERPRET,
    )(side, slots, near_small, far_small)


def grads_kernel(side, slots, small_a, small_b, data_a, data_b, out, picks, weights, both):
    count = data_a.shape[0]

    @pl.when(pl.program_id(0) == 0)
    def _():
        found, weight = row_select(side[0], slots, (small_a, small_b))
        picks[:, :count] = found[0]
        picks[:, count:] = found[1]
        weights[...] = weight

    both[:count] = data_a[...]
    both[count:] = data_b[...]
    rows = jnp.dot(picks[...], both[...], preferred_element_type=F32)
    rows = (rows * weights[...]).astype(BF16)
    for yz in range(YZ):
        out[yz] = rows[yz * PAIR : (yz + 1) * PAIR]


def grads_call(side, slots, smalls, data):
    count, width = data[0].shape
    step = width // GATHER_STEPS
    whole = lambda shape: pl.BlockSpec(shape, lambda j: (0,) * len(shape))
    rows = YZ * PAIR
    return pl.pallas_call(
        grads_kernel,
        grid=(width // step,),
        in_specs=[pl.BlockSpec(memory_space=pltpu.SMEM), whole(slots.shape)]
        + [whole(s.shape) for s in smalls]
        + [pl.BlockSpec((count, step), lambda j: (0, j)) for _ in data],
        out_specs=pl.BlockSpec((YZ, PAIR, step), lambda j: (0, 0, j)),
        out_shape=jax.ShapeDtypeStruct((YZ, PAIR, width), BF16),
        scratch_shapes=[
            pltpu.VMEM((rows, 2 * count), BF16),
            pltpu.VMEM((rows, 1), F32),
            pltpu.VMEM((2 * count, step), BF16),
        ],
        compiler_params=params(),
        cost_estimate=cost(4 * rows * count * width, 2 * width * (2 * count + rows)),
        interpret=INTERPRET,
    )(side, slots, *smalls, *data)


def tokens_kernel(near, picks, own, data_a, data_b, data_c, data_d, out, both):
    count = own.shape[0]

    @pl.when(near[0] == 1)
    def _():
        both[:count] = own[...]

    @pl.when(near[0] != 1)
    def _():
        both[:count] = data_a[...]

    both[count : 2 * count] = data_b[...]
    both[2 * count : 3 * count] = data_c[...]
    both[3 * count :] = data_d[...]
    for group in range(2):
        rows = jnp.dot(
            picks[group],
            both[2 * group * count : 2 * (group + 1) * count],
            preferred_element_type=F32,
        ).astype(BF16)
        for yz in range(YZ):
            out[yz, group * PAIR : (group + 1) * PAIR] = rows[yz * PAIR : (yz + 1) * PAIR]


def tokens_call(near, picks, data):
    count, width = data[0].shape
    step = width // GATHER_STEPS
    rows = YZ * PAIR
    return pl.pallas_call(
        tokens_kernel,
        grid=(width // step,),
        in_specs=[
            pl.BlockSpec(memory_space=pltpu.SMEM),
            pl.BlockSpec(picks.shape, lambda j: (0, 0, 0)),
        ]
        + [pl.BlockSpec((count, step), lambda j: (0, j)) for _ in data],
        out_specs=pl.BlockSpec((YZ, 2 * PAIR, step), lambda j: (0, 0, j)),
        out_shape=jax.ShapeDtypeStruct((YZ, 2 * PAIR, width), BF16),
        scratch_shapes=[pltpu.VMEM((4 * count, step), BF16)],
        compiler_params=params(),
        cost_estimate=cost(8 * rows * count * width, 2 * width * (5 * count + 2 * rows)),
        interpret=INTERPRET,
    )(near, picks, *data)


def marker_kernel(near, rows, out):
    out[0] = near[0]


def marker_call(near, rows):
    return pl.pallas_call(
        marker_kernel,
        in_specs=[
            pl.BlockSpec(memory_space=pltpu.SMEM),
            pl.BlockSpec(memory_space=pl.ANY),
        ],
        out_specs=pl.BlockSpec(memory_space=pltpu.SMEM),
        out_shape=jax.ShapeDtypeStruct((1,), jnp.int32),
        interpret=INTERPRET,
    )(near, rows)


def forward_kernel(rows, gate_up_a, gate_up_b, hidden_a, hidden_b, total):
    k = pl.program_id(0)

    @pl.when(k == 0)
    def _():
        total[...] = jnp.zeros_like(total)

    for owner, gate_up in enumerate((gate_up_a, gate_up_b)):
        weight = jnp.concatenate([gate_up[0, 0], gate_up[0, 1]], axis=1)
        total[owner] += jnp.dot(rows[...], weight, preferred_element_type=F32)

    @pl.when(k == pl.num_programs(0) - 1)
    def _():
        part = hidden_a.shape[0]
        for owner, hidden_t in enumerate((hidden_a, hidden_b)):
            gate, up = total[owner, :, :part], total[owner, :, part:]
            hidden_t[...] = jnp.transpose(gate * jax.nn.sigmoid(gate) * up).astype(BF16)


def forward_call(behind, half, rows, gate_up_a, gate_up_b):
    count, width = rows.shape
    part = gate_up_a.shape[3] // 2
    step = width // FORWARD_STEPS
    weight = pl.BlockSpec((1, 2, step, part), lambda k: (0, 0, k, half))
    whole = lambda shape: pl.BlockSpec(shape, lambda k: (0,) * len(shape))
    shapes = [((part, count), BF16), ((part, count), BF16), ((2, count, 2 * part), F32)]
    return pl.pallas_call(
        after(forward_kernel, len(behind)),
        grid=(width // step,),
        in_specs=[pl.BlockSpec(memory_space=pl.ANY) for _ in behind]
        + [pl.BlockSpec((count, step), lambda k: (0, k)), weight, weight],
        out_specs=[whole(s) for s, _ in shapes],
        out_shape=[jax.ShapeDtypeStruct(*s) for s in shapes],
        compiler_params=params(),
        cost_estimate=cost(8 * count * width * part, 2 * width * (count + 4 * part)),
        interpret=INTERPRET,
    )(*behind, rows, gate_up_a, gate_up_b)


def join(near, rows, if_near, if_not):
    for value, pieces in ((1, if_near), (0, if_not)):

        @pl.when(near[0] == value)
        def _(pieces=pieces):
            rows[:, :PAIR] = pieces[0][...]
            rows[:, PAIR:] = pieces[1][...]


def backward_kernel(
    near, own, in_12, in_3, down_a, down_b, gates_a, gates_b, back_a, back_b, rows, total
):
    k = pl.program_id(0)

    @pl.when(k == 0)
    def _():
        total[...] = jnp.zeros_like(total)

    join(near, rows, (own, in_12), (in_12, in_3))
    grads = rows[...].reshape(-1, rows.shape[2])
    for owner, down in enumerate((down_a, down_b)):
        total[owner] += lax.dot_general(
            grads, down[0], (((1,), (1,)), ((), ())), preferred_element_type=F32
        )

    @pl.when(k == pl.num_programs(0) - 1)
    def _():
        units = total.shape[2]
        part = units // 2
        for owner, back in enumerate((back_a, back_b)):
            for half, gates in enumerate((gates_a, gates_b)):
                at = half * part
                gate, up = gates[owner, :, :part], gates[owner, :, part:]
                hidden_grad = total[owner, :, at : at + part]
                sigmoid = jax.nn.sigmoid(gate)
                back[:, at : at + part] = (
                    hidden_grad * up * sigmoid * (1.0 + gate * (1.0 - sigmoid))
                ).astype(BF16)
                back[:, units + at : units + at + part] = (
                    hidden_grad * (gate * sigmoid)
                ).astype(BF16)


def backward_call(behind, near, pieces, down_a, down_b, gates):
    width = pieces[0].shape[2]
    count = 2 * YZ * PAIR
    units = down_a.shape[1]
    step = width // FORWARD_STEPS
    weight = pl.BlockSpec((1, units, step), lambda k: (0, 0, k))
    whole = lambda shape: pl.BlockSpec(shape, lambda k: (0,) * len(shape))
    return pl.pallas_call(
        after(backward_kernel, len(behind)),
        grid=(width // step,),
        in_specs=[pl.BlockSpec(memory_space=pl.ANY) for _ in behind]
        + [pl.BlockSpec(memory_space=pltpu.SMEM)]
        + [pl.BlockSpec((YZ, PAIR, step), lambda k: (0, 0, k)) for _ in pieces]
        + [weight, weight, whole(gates[0].shape), whole(gates[1].shape)],
        out_specs=[whole((count, 2 * units))] * 2,
        out_shape=[jax.ShapeDtypeStruct((count, 2 * units), BF16)] * 2,
        scratch_shapes=[
            pltpu.VMEM((YZ, 2 * PAIR, step), BF16),
            pltpu.VMEM((2, count, units), F32),
        ],
        compiler_params=params(),
        cost_estimate=cost(
            4 * count * width * units, 3 * width * count + 4 * width * units + 16 * count * units
        ),
        interpret=INTERPRET,
    )(*behind, near, *pieces, down_a, down_b, *gates)


def adam(gradient, first, second):
    first_new = 0.9 * first.astype(F32) + 0.1 * gradient
    second_new = 0.95 * second.astype(F32) + 0.05 * gradient * gradient
    return (first_new / (jnp.sqrt(second_new) + 1e-08)).astype(BF16)


def after(kernel, count):
    return lambda *refs: kernel(*refs[count:])


def down_kernel(
    near, hidden_a, hidden_b, own, in_12, in_3, core_0, core_12, core_3, first, second, out, rows
):
    width = rows.shape[3]
    join(near, rows.at[0], (own, in_12), (in_12, in_3))
    join(near, rows.at[1], (core_12, core_3), (core_0, core_12))
    gradient = jnp.dot(
        hidden_a[...], rows[0].reshape(-1, width), preferred_element_type=F32
    ) + jnp.dot(hidden_b[...], rows[1].reshape(-1, width), preferred_element_type=F32)
    out[0] = adam(gradient, first[0], second[0])


def down_call(behind, half, near, hiddens, pieces, first, second, start, units, step):
    part, count = hiddens[0].shape
    moment = pl.BlockSpec((1, part, step), lambda j: (0, half, start + j))
    whole = pl.BlockSpec((part, count), lambda j: (0, 0))
    return pl.pallas_call(
        after(down_kernel, len(behind)),
        grid=(units,),
        in_specs=[pl.BlockSpec(memory_space=pl.ANY) for _ in behind]
        + [pl.BlockSpec(memory_space=pltpu.SMEM), whole, whole]
        + [pl.BlockSpec((YZ, PAIR, step), lambda j: (0, 0, start + j)) for _ in pieces]
        + [moment, moment],
        out_specs=pl.BlockSpec((1, part, step), lambda j: (0, 0, j)),
        out_shape=jax.ShapeDtypeStruct((1, part, units * step), BF16),
        scratch_shapes=[pltpu.VMEM((2, YZ, 2 * PAIR, step), BF16)],
        compiler_params=params(),
        cost_estimate=cost(
            4 * count * part * units * step, 2 * units * step * (3 * count + 3 * part)
        ),
        interpret=INTERPRET,
    )(*behind, near, *hiddens, *pieces, first, second)


def contract_rows(left, right):
    return lax.dot_general(left, right, (((0,), (0,)), ((), ())), preferred_element_type=F32)


def gate_up_kernel(rows_a, rows_b, back_a, back_b, first, second, out):
    inner = first.shape[3]
    gradient = contract_rows(rows_a[...], back_a[...])
    gradient = gradient + contract_rows(rows_b[...], back_b[...])
    for half in range(2):
        out[0, half] = adam(
            gradient[:, half * inner : (half + 1) * inner], first[0, half], second[0, half]
        )


def gate_up_call(behind, rows, backs, first, second, start, units, step):
    count, _ = rows[0].shape
    inner = first.shape[3]
    part = pl.BlockSpec((count, step), lambda j: (0, start + j))
    moment = pl.BlockSpec((1, 2, step, inner), lambda j: (0, 0, start + j, 0))
    whole = pl.BlockSpec((count, 2 * inner), lambda j: (0, 0))
    return pl.pallas_call(
        after(gate_up_kernel, len(behind)),
        grid=(units,),
        in_specs=[pl.BlockSpec(memory_space=pl.ANY) for _ in behind]
        + [part, part, whole, whole, moment, moment],
        out_specs=pl.BlockSpec((1, 2, step, inner), lambda j: (0, 0, j, 0)),
        out_shape=jax.ShapeDtypeStruct((1, 2, units * step, inner), BF16),
        compiler_params=params(),
        cost_estimate=cost(
            8 * count * inner * units * step, 2 * units * step * (2 * count + 6 * inner)
        ),
        interpret=INTERPRET,
    )(*behind, *rows, *backs, first, second)


def place_kernel(swapping, mine, theirs, *rest):
    out = rest[-1]

    @pl.when(swapping[0] == 1)
    def _():
        out[...] = theirs[...]

    @pl.when(swapping[0] != 1)
    def _():
        out[...] = mine[...]


def place(behind, swapping, mine, theirs, whole, shape, half, start, units):
    block = tuple(n // units if k == 2 else n for k, n in enumerate(mine.shape))
    at = lambda base, row: lambda j: (0, row, base + j, 0)[: len(block)]
    old = behind + ([] if whole is None else [whole])
    return pl.pallas_call(
        place_kernel,
        grid=(units,),
        in_specs=[
            pl.BlockSpec(memory_space=pltpu.SMEM),
            pl.BlockSpec(block, at(0, 0)),
            pl.BlockSpec(block, at(0, 0)),
        ]
        + [pl.BlockSpec(memory_space=pl.ANY) for _ in old],
        out_specs=pl.BlockSpec(block, at(start, half)),
        out_shape=jax.ShapeDtypeStruct(shape, BF16),
        input_output_aliases={} if whole is None else {2 + len(old): 0},
        compiler_params=params(),
        cost_estimate=cost(0, 6 * mine.size),
        interpret=INTERPRET,
    )(swapping, mine, theirs, *old)


def local(
    tokens,
    cotangent,
    expert_ids,
    combine,
    slot_expert,
    swap_flag,
    w_gate_up,
    w_down,
    first_gate_up,
    first_down,
    second_gate_up,
    second_down,
):
    width = tokens.shape[1]
    core = lax.axis_index("dp") % 2
    my_slot = lax.axis_index("expert")
    side = my_slot % 2
    near = (core == side).astype(jnp.int32)
    slots = slot_expert[None, :]
    small = jnp.concatenate([expert_ids.T.astype(F32), combine.T], axis=0)
    token_goals = (token_1, token_2, token_3, token_4)

    small_core = send(small, to_core)
    cotangent_core = send(cotangent, to_core)
    tokens_in = [send(tokens, t) for t in token_goals]
    near = near.reshape(1)
    scaled = grads_call(
        core.astype(jnp.int32).reshape(1), slots, [small, small_core], [cotangent, cotangent_core]
    )
    grads_0 = over_yz(scaled)
    down_core = send(w_down, to_core)
    gate_up_core = send(w_gate_up, to_core)

    chip = jnp.concatenate([small, small_core], axis=0)
    small_a = send(chip, small_near)
    small_b = send(chip, token_3)
    small_a = jnp.where(near == 1, chip, small_a)
    picks = picks_call(side.astype(jnp.int32).reshape(1), slots, small_a, small_b)
    sent_rows = tokens_call(near, picks, [tokens] + tokens_in)
    grads_12 = send(grads_0, grad_12)
    grads_3 = send(grads_0, grad_3)
    core_0 = send(grads_0, grad_near)
    rows_a = over_yz(sent_rows).reshape(-1, width)
    marked = marker_call(near, rows_a)
    core_12 = send(grads_12, to_core)
    core_3 = send(grads_3, grad_far)
    mine_in = [grads_0, grads_12, grads_3]
    rows_b = send(rows_a, to_core)

    swapping = swap_flag[my_slot].reshape(1)
    pending, behind, gates, step = [], [], [], width // 7
    for half, parts in enumerate(((2, 5), (7,))):
        hidden_a, hidden_other, gate = forward_call(behind, half, rows_a, w_gate_up, gate_up_core)
        gates.append(gate)
        hidden_b = send(hidden_other, to_core)
        start = 0
        for units in parts:
            mine = down_call(
                behind,
                half,
                marked,
                (hidden_a, hidden_b),
                mine_in + [core_0, core_12, core_3],
                first_down,
                second_down,
                start,
                units,
                step,
            )
            theirs = send(mine, to_swap)
            pending.append((mine, theirs, half, start, units))
            behind, start = [mine], start + units
    downs = len(pending)
    back_a, back_other = backward_call(behind, marked, mine_in, w_down, down_core, gates)
    back_b = send(back_other, to_core)
    start, step = 0, width // 14
    for units in (4, 4, 4, 1, 1):
        mine = gate_up_call(
            behind,
            (rows_a, rows_b),
            (back_a, back_b),
            first_gate_up,
            second_gate_up,
            start,
            units,
            step,
        )
        theirs = send(mine, to_swap)
        pending.append((mine, theirs, 0, start, units))
        behind, start = [mine], start + units
    whole = None
    for mine, theirs, half, start, units in pending[:downs]:
        whole = place([], swapping, mine, theirs, whole, w_down.shape, half, start, units)
    step_down, whole, behind = whole, None, [whole]
    for mine, theirs, half, start, units in pending[downs:]:
        whole = place(
            behind, swapping, mine, theirs, whole, w_gate_up.shape, half, start, units
        )
        behind = []
    return (whole, step_down)


def solution(mesh):
    return jax.shard_map(
        local,
        mesh=mesh,
        in_specs=(
            P(("dp", "expert"), None),
            P(("dp", "expert"), None),
            P(("dp", "expert"), None),
            P(("dp", "expert"), None),
            P(),
            P(),
            P("expert", None, None, "dp"),
            P("expert", "dp", None),
            P("expert", None, None, "dp"),
            P("expert", "dp", None),
            P("expert", None, None, "dp"),
            P("expert", "dp", None),
        ),
        out_specs=(P("expert", None, None, "dp"), P("expert", "dp", None)),
        check_vma=False,
    )
```

```python
import jax
import jax.numpy as jnp
from jax import lax
from jax.experimental import pallas as pl
from jax.experimental.pallas import tpu as pltpu
from jax.sharding import PartitionSpec as P


INTERPRET = False
AXES = ("dp", "expert")
YZ = 16
CAP = 12
PAIR = 2 * CAP
GATHER_STEPS = 2
FORWARD_STEPS = 4
F32 = jnp.float32
BF16 = jnp.bfloat16


def device_id(xl, c, yz, xh):
    return ((xl * 2 + c) * YZ + yz) * 2 + xh


def send(value, target):
    pairs = []
    for xl in range(2):
        for c in range(2):
            for yz in range(YZ):
                for xh in range(2):
                    goal = target(xl, c, yz, xh)
                    if goal is not None:
                        pairs.append((device_id(xl, c, yz, xh), device_id(*goal)))
    return lax.ppermute(value, AXES, pairs)


def to_core(xl, c, yz, xh):
    return (xl, 1 - c, yz, xh)


def to_swap(xl, c, yz, xh):
    return (xl, c, yz ^ (YZ // 2), xh)


def token_1(xl, c, yz, xh):
    return None if c == xh else (1 - xl, 1 - c, yz, 1 - xh)


def token_2(xl, c, yz, xh):
    return (1 - xl, c, yz, 1 - xh) if c == xh else (xl, 1 - c, yz, xh)


def token_3(xl, c, yz, xh):
    return (1 - xl, c, yz, xh) if c == xh else (xl, 1 - c, yz, 1 - xh)


def token_4(xl, c, yz, xh):
    return (xl, c, yz, 1 - xh) if c == xh else (1 - xl, 1 - c, yz, xh)


def grad_near(xl, c, yz, xh):
    return (xl, 1 - c, yz, xh) if c == xh else None


def grad_far(xl, c, yz, xh):
    return None if c == xh else (xl, 1 - c, yz, xh)


def small_near(xl, c, yz, xh):
    return None if c == xh else (1 - xl, 1 - c, yz, 1 - xh)


def grad_12(xl, c, yz, xh):
    return (1 - xl, c, yz, xh) if c == xh else (1 - xl, 1 - c, yz, 1 - xh)


def grad_3(xl, c, yz, xh):
    return None if c == xh else (xl, 1 - c, yz, 1 - xh)


def over_yz(value):
    groups = [[yz * 2 + xh for yz in range(YZ)] for xh in range(2)]
    return lax.all_to_all(value, "expert", 0, 0, axis_index_groups=groups, tiled=True)


def params(count=1):
    return pltpu.CompilerParams(
        dimension_semantics=("arbitrary",) * count
    )


def cost(flops, size):
    return pl.CostEstimate(flops=int(flops), bytes_accessed=int(size), transcendentals=0)


def row_select(side, slots_ref, small_refs):
    rows = YZ * PAIR
    tokens = small_refs[0].shape[1]
    row = lax.broadcasted_iota(jnp.int32, (rows, 1), 0).astype(F32)
    twelve = jnp.floor((row + 0.5) * (1.0 / CAP))
    place = row - twelve * CAP
    dest = jnp.floor((twelve + 0.5) * 0.5)
    block = twelve - dest * 2
    slots = slots_ref[...].astype(F32)
    lane = lax.broadcasted_iota(jnp.int32, (rows, slots.shape[1]), 1).astype(F32)
    named = jnp.sum(
        jnp.where(lane == dest * 2 + side.astype(F32), slots, 0.0), axis=1, keepdims=True
    )
    before = lax.broadcasted_iota(jnp.int32, (tokens, tokens), 0)
    after = lax.broadcasted_iota(jnp.int32, (tokens, tokens), 1)
    earlier = jnp.where(before < after, 1.0, 0.0).astype(BF16)
    picks, weight = [], jnp.zeros((rows, 1), F32)
    for b, small in enumerate(small_refs):
        first = small[0:1, :] == named
        second = small[1:2, :] == named
        hit = jnp.where(first, 1.0, jnp.where(second, 1.0, 0.0))
        position = jnp.dot(hit.astype(BF16), earlier, preferred_element_type=F32)
        wanted = jnp.where(block == float(b), place, -1.0)
        pick = jnp.where(position == wanted, hit, 0.0)
        share = jnp.where(first, small[2:3, :], small[3:4, :])
        weight = weight + jnp.sum(pick * share, axis=1, keepdims=True)
        picks.append(pick.astype(BF16))
    return picks, weight


def picks_kernel(side, slots, near_small, far_small, out):
    tokens = near_small.shape[1]
    for group, small in enumerate((near_small[...], far_small[...])):
        half = small.shape[0] // 2
        found, _ = row_select(side[0], slots, (small[:half], small[half:]))
        out[group, :, :tokens] = found[0]
        out[group, :, tokens:] = found[1]


def picks_call(side, slots, near_small, far_small):
    return pl.pallas_call(
        picks_kernel,
        in_specs=[pl.BlockSpec(memory_space=pltpu.SMEM)]
        + [pl.BlockSpec(memory_space=pltpu.VMEM)] * 3,
        out_specs=pl.BlockSpec(memory_space=pltpu.VMEM),
        out_shape=jax.ShapeDtypeStruct((2, YZ * PAIR, 2 * near_small.shape[1]), BF16),
        cost_estimate=cost(10**8, 10**6),
        interpret=INTERPRET,
    )(side, slots, near_small, far_small)


def grads_kernel(side, slots, small_a, small_b, data_a, data_b, out, picks, weights, both):
    count = data_a.shape[0]

    @pl.when(pl.program_id(0) == 0)
    def _():
        found, weight = row_select(side[0], slots, (small_a, small_b))
        picks[:, :count] = found[0]
        picks[:, count:] = found[1]
        weights[...] = weight

    both[:count] = data_a[...]
    both[count:] = data_b[...]
    rows = jnp.dot(picks[...], both[...], preferred_element_type=F32)
    rows = (rows * weights[...]).astype(BF16)
    for yz in range(YZ):
        out[yz] = rows[yz * PAIR : (yz + 1) * PAIR]


def grads_call(side, slots, smalls, data):
    count, width = data[0].shape
    step = width // GATHER_STEPS
    whole = lambda shape: pl.BlockSpec(shape, lambda j: (0,) * len(shape))
    rows = YZ * PAIR
    return pl.pallas_call(
        grads_kernel,
        grid=(width // step,),
        in_specs=[pl.BlockSpec(memory_space=pltpu.SMEM), whole(slots.shape)]
        + [whole(s.shape) for s in smalls]
        + [pl.BlockSpec((count, step), lambda j: (0, j)) for _ in data],
        out_specs=pl.BlockSpec((YZ, PAIR, step), lambda j: (0, 0, j)),
        out_shape=jax.ShapeDtypeStruct((YZ, PAIR, width), BF16),
        scratch_shapes=[
            pltpu.VMEM((rows, 2 * count), BF16),
            pltpu.VMEM((rows, 1), F32),
            pltpu.VMEM((2 * count, step), BF16),
        ],
        compiler_params=params(),
        cost_estimate=cost(4 * rows * count * width, 2 * width * (2 * count + rows)),
        interpret=INTERPRET,
    )(side, slots, *smalls, *data)


def tokens_kernel(near, picks, own, data_a, data_b, data_c, data_d, out, both):
    count = own.shape[0]

    @pl.when(near[0] == 1)
    def _():
        both[:count] = own[...]

    @pl.when(near[0] != 1)
    def _():
        both[:count] = data_a[...]

    both[count : 2 * count] = data_b[...]
    both[2 * count : 3 * count] = data_c[...]
    both[3 * count :] = data_d[...]
    for group in range(2):
        rows = jnp.dot(
            picks[group],
            both[2 * group * count : 2 * (group + 1) * count],
            preferred_element_type=F32,
        ).astype(BF16)
        for yz in range(YZ):
            out[yz, group * PAIR : (group + 1) * PAIR] = rows[yz * PAIR : (yz + 1) * PAIR]


def tokens_call(near, picks, data):
    count, width = data[0].shape
    step = width // GATHER_STEPS
    rows = YZ * PAIR
    return pl.pallas_call(
        tokens_kernel,
        grid=(width // step,),
        in_specs=[
            pl.BlockSpec(memory_space=pltpu.SMEM),
            pl.BlockSpec(picks.shape, lambda j: (0, 0, 0)),
        ]
        + [pl.BlockSpec((count, step), lambda j: (0, j)) for _ in data],
        out_specs=pl.BlockSpec((YZ, 2 * PAIR, step), lambda j: (0, 0, j)),
        out_shape=jax.ShapeDtypeStruct((YZ, 2 * PAIR, width), BF16),
        scratch_shapes=[pltpu.VMEM((4 * count, step), BF16)],
        compiler_params=params(),
        cost_estimate=cost(8 * rows * count * width, 2 * width * (5 * count + 2 * rows)),
        interpret=INTERPRET,
    )(near, picks, *data)


def marker_kernel(near, rows, out):
    out[0] = near[0]


def marker_call(near, rows):
    return pl.pallas_call(
        marker_kernel,
        in_specs=[
            pl.BlockSpec(memory_space=pltpu.SMEM),
            pl.BlockSpec(memory_space=pl.ANY),
        ],
        out_specs=pl.BlockSpec(memory_space=pltpu.SMEM),
        out_shape=jax.ShapeDtypeStruct((1,), jnp.int32),
        interpret=INTERPRET,
    )(near, rows)


def forward_kernel(rows, gate_up_a, gate_up_b, hidden_a, hidden_b, total):
    k = pl.program_id(0)

    @pl.when(k == 0)
    def _():
        total[...] = jnp.zeros_like(total)

    for owner, gate_up in enumerate((gate_up_a, gate_up_b)):
        weight = jnp.concatenate([gate_up[0, 0], gate_up[0, 1]], axis=1)
        total[owner] += jnp.dot(rows[...], weight, preferred_element_type=F32)

    @pl.when(k == pl.num_programs(0) - 1)
    def _():
        part = hidden_a.shape[0]
        for owner, hidden_t in enumerate((hidden_a, hidden_b)):
            gate, up = total[owner, :, :part], total[owner, :, part:]
            hidden_t[...] = jnp.transpose(gate * jax.nn.sigmoid(gate) * up).astype(BF16)


def forward_call(rows, gate_up_a, gate_up_b):
    count, width = rows.shape
    part = gate_up_a.shape[3]
    step = width // FORWARD_STEPS
    weight = pl.BlockSpec((1, 2, step, part), lambda k: (0, 0, k, 0))
    whole = lambda shape: pl.BlockSpec(shape, lambda k: (0,) * len(shape))
    shapes = [((part, count), BF16), ((part, count), BF16), ((2, count, 2 * part), F32)]
    return pl.pallas_call(
        forward_kernel,
        grid=(width // step,),
        in_specs=[pl.BlockSpec((count, step), lambda k: (0, k)), weight, weight],
        out_specs=[whole(s) for s, _ in shapes],
        out_shape=[jax.ShapeDtypeStruct(*s) for s in shapes],
        compiler_params=params(),
        cost_estimate=cost(8 * count * width * part, 2 * width * (count + 4 * part)),
        interpret=INTERPRET,
    )(rows, gate_up_a, gate_up_b)


def join(near, rows, if_near, if_not):
    for value, pieces in ((1, if_near), (0, if_not)):

        @pl.when(near[0] == value)
        def _(pieces=pieces):
            rows[:, :PAIR] = pieces[0][...]
            rows[:, PAIR:] = pieces[1][...]


def backward_kernel(
    near, own, in_12, in_3, down_a, down_b, gates, back_a, back_b, rows, total
):
    k = pl.program_id(0)

    @pl.when(k == 0)
    def _():
        total[...] = jnp.zeros_like(total)

    join(near, rows, (own, in_12), (in_12, in_3))
    grads = rows[...].reshape(-1, rows.shape[2])
    for owner, down in enumerate((down_a, down_b)):
        total[owner] += lax.dot_general(
            grads, down[0], (((1,), (1,)), ((), ())), preferred_element_type=F32
        )

    @pl.when(k == pl.num_programs(0) - 1)
    def _():
        units = total.shape[2]
        for owner, back in enumerate((back_a, back_b)):
            gate, up = gates[owner, :, :units], gates[owner, :, units:]
            hidden_grad = total[owner]
            sigmoid = jax.nn.sigmoid(gate)
            back[:, :units] = (
                hidden_grad * up * sigmoid * (1.0 + gate * (1.0 - sigmoid))
            ).astype(BF16)
            back[:, units:] = (hidden_grad * (gate * sigmoid)).astype(BF16)


def backward_call(behind, near, pieces, down_a, down_b, gates):
    width = pieces[0].shape[2]
    count = 2 * YZ * PAIR
    units = down_a.shape[1]
    step = width // FORWARD_STEPS
    weight = pl.BlockSpec((1, units, step), lambda k: (0, 0, k))
    whole = lambda shape: pl.BlockSpec(shape, lambda k: (0,) * len(shape))
    return pl.pallas_call(
        after(backward_kernel, len(behind)),
        grid=(width // step,),
        in_specs=[pl.BlockSpec(memory_space=pl.ANY) for _ in behind]
        + [pl.BlockSpec(memory_space=pltpu.SMEM)]
        + [pl.BlockSpec((YZ, PAIR, step), lambda k: (0, 0, k)) for _ in pieces]
        + [weight, weight, whole(gates.shape)],
        out_specs=[whole((count, 2 * units))] * 2,
        out_shape=[jax.ShapeDtypeStruct((count, 2 * units), BF16)] * 2,
        scratch_shapes=[
            pltpu.VMEM((YZ, 2 * PAIR, step), BF16),
            pltpu.VMEM((2, count, units), F32),
        ],
        compiler_params=params(),
        cost_estimate=cost(
            4 * count * width * units, 3 * width * count + 4 * width * units + 16 * count * units
        ),
        interpret=INTERPRET,
    )(*behind, near, *pieces, down_a, down_b, gates)


def adam(gradient, first, second):
    first_new = 0.9 * first.astype(F32) + 0.1 * gradient
    second_new = 0.95 * second.astype(F32) + 0.05 * gradient * gradient
    return (first_new / (jnp.sqrt(second_new) + 1e-08)).astype(BF16)


def after(kernel, count):
    return lambda *refs: kernel(*refs[count:])


def down_kernel(
    near, hidden_a, hidden_b, own, in_12, in_3, core_0, core_12, core_3, first, second, out, rows
):
    width = rows.shape[3]
    join(near, rows.at[0], (own, in_12), (in_12, in_3))
    join(near, rows.at[1], (core_12, core_3), (core_0, core_12))
    gradient = jnp.dot(
        hidden_a[...], rows[0].reshape(-1, width), preferred_element_type=F32
    ) + jnp.dot(hidden_b[...], rows[1].reshape(-1, width), preferred_element_type=F32)
    out[0] = adam(gradient, first[0], second[0])


def down_call(behind, near, hiddens, pieces, first, second, start, units, step):
    part, count = hiddens[0].shape
    moment = pl.BlockSpec((1, part, step), lambda j: (0, 0, start + j))
    whole = pl.BlockSpec((part, count), lambda j: (0, 0))
    return pl.pallas_call(
        after(down_kernel, len(behind)),
        grid=(units,),
        in_specs=[pl.BlockSpec(memory_space=pl.ANY) for _ in behind]
        + [pl.BlockSpec(memory_space=pltpu.SMEM), whole, whole]
        + [pl.BlockSpec((YZ, PAIR, step), lambda j: (0, 0, start + j)) for _ in pieces]
        + [moment, moment],
        out_specs=pl.BlockSpec((1, part, step), lambda j: (0, 0, j)),
        out_shape=jax.ShapeDtypeStruct((1, part, units * step), BF16),
        scratch_shapes=[pltpu.VMEM((2, YZ, 2 * PAIR, step), BF16)],
        compiler_params=params(),
        cost_estimate=cost(
            4 * count * part * units * step, 2 * units * step * (3 * count + 3 * part)
        ),
        interpret=INTERPRET,
    )(*behind, near, *hiddens, *pieces, first, second)


def contract_rows(left, right):
    return lax.dot_general(left, right, (((0,), (0,)), ((), ())), preferred_element_type=F32)


def gate_up_kernel(rows_a, rows_b, back_a, back_b, first, second, out):
    inner = first.shape[3]
    gradient = contract_rows(rows_a[...], back_a[...])
    gradient = gradient + contract_rows(rows_b[...], back_b[...])
    for half in range(2):
        out[0, half] = adam(
            gradient[:, half * inner : (half + 1) * inner], first[0, half], second[0, half]
        )


def gate_up_call(behind, rows, backs, first, second, start, units, step):
    count, _ = rows[0].shape
    inner = first.shape[3]
    part = pl.BlockSpec((count, step), lambda j: (0, start + j))
    moment = pl.BlockSpec((1, 2, step, inner), lambda j: (0, 0, start + j, 0))
    whole = pl.BlockSpec((count, 2 * inner), lambda j: (0, 0))
    return pl.pallas_call(
        after(gate_up_kernel, len(behind)),
        grid=(units,),
        in_specs=[pl.BlockSpec(memory_space=pl.ANY) for _ in behind]
        + [part, part, whole, whole, moment, moment],
        out_specs=pl.BlockSpec((1, 2, step, inner), lambda j: (0, 0, j, 0)),
        out_shape=jax.ShapeDtypeStruct((1, 2, units * step, inner), BF16),
        compiler_params=params(),
        cost_estimate=cost(
            8 * count * inner * units * step, 2 * units * step * (2 * count + 6 * inner)
        ),
        interpret=INTERPRET,
    )(*behind, *rows, *backs, first, second)


def place_kernel(swapping, mine, theirs, *rest):
    out = rest[-1]

    @pl.when(swapping[0] == 1)
    def _():
        out[...] = theirs[...]

    @pl.when(swapping[0] != 1)
    def _():
        out[...] = mine[...]


def place(behind, swapping, mine, theirs, whole, shape, start, units):
    block = tuple(n // units if k == 2 else n for k, n in enumerate(mine.shape))
    at = lambda base: lambda j: (0, 0, base + j, 0)[: len(block)]
    old = behind + ([] if whole is None else [whole])
    return pl.pallas_call(
        place_kernel,
        grid=(units,),
        in_specs=[
            pl.BlockSpec(memory_space=pltpu.SMEM),
            pl.BlockSpec(block, at(0)),
            pl.BlockSpec(block, at(0)),
        ]
        + [pl.BlockSpec(memory_space=pl.ANY) for _ in old],
        out_specs=pl.BlockSpec(block, at(start)),
        out_shape=jax.ShapeDtypeStruct(shape, BF16),
        input_output_aliases={} if whole is None else {2 + len(old): 0},
        compiler_params=params(),
        cost_estimate=cost(0, 6 * mine.size),
        interpret=INTERPRET,
    )(swapping, mine, theirs, *old)


def local(
    tokens,
    cotangent,
    expert_ids,
    combine,
    slot_expert,
    swap_flag,
    w_gate_up,
    w_down,
    first_gate_up,
    first_down,
    second_gate_up,
    second_down,
):
    width = tokens.shape[1]
    core = lax.axis_index("dp") % 2
    my_slot = lax.axis_index("expert")
    side = my_slot % 2
    near = (core == side).astype(jnp.int32)
    slots = slot_expert[None, :]
    small = jnp.concatenate([expert_ids.T.astype(F32), combine.T], axis=0)
    token_goals = (token_1, token_2, token_3, token_4)

    small_core = send(small, to_core)
    cotangent_core = send(cotangent, to_core)
    tokens_in = [send(tokens, t) for t in token_goals]
    near = near.reshape(1)
    scaled = grads_call(
        core.astype(jnp.int32).reshape(1), slots, [small, small_core], [cotangent, cotangent_core]
    )
    grads_0 = over_yz(scaled)
    down_core = send(w_down, to_core)
    gate_up_core = send(w_gate_up, to_core)

    chip = jnp.concatenate([small, small_core], axis=0)
    small_a = send(chip, small_near)
    small_b = send(chip, token_3)
    small_a = jnp.where(near == 1, chip, small_a)
    picks = picks_call(side.astype(jnp.int32).reshape(1), slots, small_a, small_b)
    sent_rows = tokens_call(near, picks, [tokens] + tokens_in)
    grads_12 = send(grads_0, grad_12)
    grads_3 = send(grads_0, grad_3)
    core_0 = send(grads_0, grad_near)
    rows_a = over_yz(sent_rows).reshape(-1, width)
    marked = marker_call(near, rows_a)
    core_12 = send(grads_12, to_core)
    core_3 = send(grads_3, grad_far)
    mine_in = [grads_0, grads_12, grads_3]
    rows_b = send(rows_a, to_core)

    swapping = swap_flag[my_slot].reshape(1)
    pending, behind, start, step = [], [], 0, width // 7
    hidden_a, hidden_other, gates = forward_call(rows_a, w_gate_up, gate_up_core)
    hidden_b = send(hidden_other, to_core)
    for units in (1, 2, 4):
        mine = down_call(
            behind,
            marked,
            (hidden_a, hidden_b),
            mine_in + [core_0, core_12, core_3],
            first_down,
            second_down,
            start,
            units,
            step,
        )
        theirs = send(mine, to_swap)
        pending.append((mine, theirs, start, units))
        behind, start = [mine], start + units
    downs = len(pending)
    back_a, back_other = backward_call(behind, marked, mine_in, w_down, down_core, gates)
    back_b = send(back_other, to_core)
    start, step = 0, width // 14
    for units in (4, 4, 4, 1, 1):
        mine = gate_up_call(
            behind,
            (rows_a, rows_b),
            (back_a, back_b),
            first_gate_up,
            second_gate_up,
            start,
            units,
            step,
        )
        theirs = send(mine, to_swap)
        pending.append((mine, theirs, start, units))
        behind, start = [mine], start + units
    whole = None
    for mine, theirs, start, units in pending[:downs]:
        whole = place([], swapping, mine, theirs, whole, w_down.shape, start, units)
    step_down, whole, behind = whole, None, [whole]
    for mine, theirs, start, units in pending[downs:]:
        whole = place(behind, swapping, mine, theirs, whole, w_gate_up.shape, start, units)
        behind = []
    return (whole, step_down)


def solution(mesh):
    return jax.shard_map(
        local,
        mesh=mesh,
        in_specs=(
            P(("dp", "expert"), None),
            P(("dp", "expert"), None),
            P(("dp", "expert"), None),
            P(("dp", "expert"), None),
            P(),
            P(),
            P("expert", None, None, "dp"),
            P("expert", "dp", None),
            P("expert", None, None, "dp"),
            P("expert", "dp", None),
            P("expert", None, None, "dp"),
            P("expert", "dp", None),
        ),
        out_specs=(P("expert", None, None, "dp"), P("expert", "dp", None)),
        check_vma=False,
    )
```

```python
import jax
import jax.numpy as jnp
from jax import lax
from jax.experimental import pallas as pl
from jax.experimental.pallas import tpu as pltpu
from jax.sharding import PartitionSpec as P


INTERPRET = False
AXES = ("dp", "expert")
YZ = 16
CAP = 12
PAIR = 2 * CAP
GATHER_STEPS = 2
FORWARD_STEPS = 4
F32 = jnp.float32
BF16 = jnp.bfloat16


def device_id(xl, c, yz, xh):
    return ((xl * 2 + c) * YZ + yz) * 2 + xh


def send(value, target):
    pairs = []
    for xl in range(2):
        for c in range(2):
            for yz in range(YZ):
                for xh in range(2):
                    goal = target(xl, c, yz, xh)
                    if goal is not None:
                        pairs.append((device_id(xl, c, yz, xh), device_id(*goal)))
    return lax.ppermute(value, AXES, pairs)


def to_core(xl, c, yz, xh):
    return (xl, 1 - c, yz, xh)


def to_swap(xl, c, yz, xh):
    return (xl, c, yz ^ (YZ // 2), xh)


def token_1(xl, c, yz, xh):
    return None if c == xh else (1 - xl, 1 - c, yz, 1 - xh)


def token_2(xl, c, yz, xh):
    return (1 - xl, c, yz, 1 - xh) if c == xh else (xl, 1 - c, yz, xh)


def token_3(xl, c, yz, xh):
    return (1 - xl, c, yz, xh) if c == xh else (xl, 1 - c, yz, 1 - xh)


def token_4(xl, c, yz, xh):
    return (xl, c, yz, 1 - xh) if c == xh else (1 - xl, 1 - c, yz, xh)


def small_near(xl, c, yz, xh):
    return None if c == xh else (1 - xl, 1 - c, yz, 1 - xh)


def grad_12(xl, c, yz, xh):
    return (1 - xl, c, yz, xh) if c == xh else (1 - xl, 1 - c, yz, 1 - xh)


def grad_3(xl, c, yz, xh):
    return None if c == xh else (xl, 1 - c, yz, 1 - xh)


def over_yz(value):
    groups = [[yz * 2 + xh for yz in range(YZ)] for xh in range(2)]
    return lax.all_to_all(value, "expert", 0, 0, axis_index_groups=groups, tiled=True)


def params(count=1):
    return pltpu.CompilerParams(
        dimension_semantics=("arbitrary",) * count
    )


def cost(flops, size):
    return pl.CostEstimate(flops=int(flops), bytes_accessed=int(size), transcendentals=0)


def row_select(side, slots_ref, small_refs):
    rows = YZ * PAIR
    tokens = small_refs[0].shape[1]
    row = lax.broadcasted_iota(jnp.int32, (rows, 1), 0).astype(F32)
    twelve = jnp.floor((row + 0.5) * (1.0 / CAP))
    place = row - twelve * CAP
    dest = jnp.floor((twelve + 0.5) * 0.5)
    block = twelve - dest * 2
    slots = slots_ref[...].astype(F32)
    lane = lax.broadcasted_iota(jnp.int32, (rows, slots.shape[1]), 1).astype(F32)
    named = jnp.sum(
        jnp.where(lane == dest * 2 + side.astype(F32), slots, 0.0), axis=1, keepdims=True
    )
    before = lax.broadcasted_iota(jnp.int32, (tokens, tokens), 0)
    after = lax.broadcasted_iota(jnp.int32, (tokens, tokens), 1)
    earlier = jnp.where(before < after, 1.0, 0.0).astype(BF16)
    picks, weight = [], jnp.zeros((rows, 1), F32)
    for b, small in enumerate(small_refs):
        first = small[0:1, :] == named
        second = small[1:2, :] == named
        hit = jnp.where(first, 1.0, jnp.where(second, 1.0, 0.0))
        position = jnp.dot(hit.astype(BF16), earlier, preferred_element_type=F32)
        wanted = jnp.where(block == float(b), place, -1.0)
        pick = jnp.where(position == wanted, hit, 0.0)
        share = jnp.where(first, small[2:3, :], small[3:4, :])
        weight = weight + jnp.sum(pick * share, axis=1, keepdims=True)
        picks.append(pick.astype(BF16))
    return picks, weight


def picks_kernel(side, slots, near_small, far_small, out):
    tokens = near_small.shape[1]
    for group, small in enumerate((near_small[...], far_small[...])):
        half = small.shape[0] // 2
        found, _ = row_select(side[0], slots, (small[:half], small[half:]))
        out[group, :, :tokens] = found[0]
        out[group, :, tokens:] = found[1]


def picks_call(side, slots, near_small, far_small):
    return pl.pallas_call(
        picks_kernel,
        in_specs=[pl.BlockSpec(memory_space=pltpu.SMEM)]
        + [pl.BlockSpec(memory_space=pltpu.VMEM)] * 3,
        out_specs=pl.BlockSpec(memory_space=pltpu.VMEM),
        out_shape=jax.ShapeDtypeStruct((2, YZ * PAIR, 2 * near_small.shape[1]), BF16),
        cost_estimate=cost(10**8, 10**6),
        interpret=INTERPRET,
    )(side, slots, near_small, far_small)


def grads_kernel(side, slots, small_a, small_b, data_a, data_b, out, picks, weights, both):
    count = data_a.shape[0]

    @pl.when(pl.program_id(0) == 0)
    def _():
        found, weight = row_select(side[0], slots, (small_a, small_b))
        picks[:, :count] = found[0]
        picks[:, count:] = found[1]
        weights[...] = weight

    both[:count] = data_a[...]
    both[count:] = data_b[...]
    rows = jnp.dot(picks[...], both[...], preferred_element_type=F32)
    rows = (rows * weights[...]).astype(BF16)
    for yz in range(YZ):
        out[yz] = rows[yz * PAIR : (yz + 1) * PAIR]


def grads_call(side, slots, smalls, data):
    count, width = data[0].shape
    step = width // GATHER_STEPS
    whole = lambda shape: pl.BlockSpec(shape, lambda j: (0,) * len(shape))
    rows = YZ * PAIR
    return pl.pallas_call(
        grads_kernel,
        grid=(width // step,),
        in_specs=[pl.BlockSpec(memory_space=pltpu.SMEM), whole(slots.shape)]
        + [whole(s.shape) for s in smalls]
        + [pl.BlockSpec((count, step), lambda j: (0, j)) for _ in data],
        out_specs=pl.BlockSpec((YZ, PAIR, step), lambda j: (0, 0, j)),
        out_shape=jax.ShapeDtypeStruct((YZ, PAIR, width), BF16),
        scratch_shapes=[
            pltpu.VMEM((rows, 2 * count), BF16),
            pltpu.VMEM((rows, 1), F32),
            pltpu.VMEM((2 * count, step), BF16),
        ],
        compiler_params=params(),
        cost_estimate=cost(4 * rows * count * width, 2 * width * (2 * count + rows)),
        interpret=INTERPRET,
    )(side, slots, *smalls, *data)


def tokens_kernel(near, picks, own, data_a, data_b, data_c, data_d, out, both):
    count = own.shape[0]

    @pl.when(near[0] == 1)
    def _():
        both[:count] = own[...]

    @pl.when(near[0] != 1)
    def _():
        both[:count] = data_a[...]

    both[count : 2 * count] = data_b[...]
    both[2 * count : 3 * count] = data_c[...]
    both[3 * count :] = data_d[...]
    for group in range(2):
        rows = jnp.dot(
            picks[group],
            both[2 * group * count : 2 * (group + 1) * count],
            preferred_element_type=F32,
        ).astype(BF16)
        for yz in range(YZ):
            out[yz, group * PAIR : (group + 1) * PAIR] = rows[yz * PAIR : (yz + 1) * PAIR]


def tokens_call(near, picks, data):
    count, width = data[0].shape
    step = width // GATHER_STEPS
    rows = YZ * PAIR
    return pl.pallas_call(
        tokens_kernel,
        grid=(width // step,),
        in_specs=[
            pl.BlockSpec(memory_space=pltpu.SMEM),
            pl.BlockSpec(picks.shape, lambda j: (0, 0, 0)),
        ]
        + [pl.BlockSpec((count, step), lambda j: (0, j)) for _ in data],
        out_specs=pl.BlockSpec((YZ, 2 * PAIR, step), lambda j: (0, 0, j)),
        out_shape=jax.ShapeDtypeStruct((YZ, 2 * PAIR, width), BF16),
        scratch_shapes=[pltpu.VMEM((4 * count, step), BF16)],
        compiler_params=params(),
        cost_estimate=cost(8 * rows * count * width, 2 * width * (5 * count + 2 * rows)),
        interpret=INTERPRET,
    )(near, picks, *data)


def marker_kernel(near, rows, out):
    out[0] = near[0]


def marker_call(near, rows):
    return pl.pallas_call(
        marker_kernel,
        in_specs=[
            pl.BlockSpec(memory_space=pltpu.SMEM),
            pl.BlockSpec(memory_space=pl.ANY),
        ],
        out_specs=pl.BlockSpec(memory_space=pltpu.SMEM),
        out_shape=jax.ShapeDtypeStruct((1,), jnp.int32),
        interpret=INTERPRET,
    )(near, rows)


def forward_kernel(rows, gate_up_a, gate_up_b, hidden_a, hidden_b, total):
    k = pl.program_id(0)

    @pl.when(k == 0)
    def _():
        total[...] = jnp.zeros_like(total)

    for owner, gate_up in enumerate((gate_up_a, gate_up_b)):
        weight = jnp.concatenate([gate_up[0, 0], gate_up[0, 1]], axis=1)
        total[owner] += jnp.dot(rows[...], weight, preferred_element_type=F32)

    @pl.when(k == pl.num_programs(0) - 1)
    def _():
        part = hidden_a.shape[0]
        for owner, hidden_t in enumerate((hidden_a, hidden_b)):
            gate, up = total[owner, :, :part], total[owner, :, part:]
            hidden_t[...] = jnp.transpose(gate * jax.nn.sigmoid(gate) * up).astype(BF16)


def forward_call(rows, gate_up_a, gate_up_b):
    count, width = rows.shape
    part = gate_up_a.shape[3]
    step = width // FORWARD_STEPS
    weight = pl.BlockSpec((1, 2, step, part), lambda k: (0, 0, k, 0))
    whole = lambda shape: pl.BlockSpec(shape, lambda k: (0,) * len(shape))
    shapes = [((part, count), BF16), ((part, count), BF16), ((2, count, 2 * part), F32)]
    return pl.pallas_call(
        forward_kernel,
        grid=(width // step,),
        in_specs=[pl.BlockSpec((count, step), lambda k: (0, k)), weight, weight],
        out_specs=[whole(s) for s, _ in shapes],
        out_shape=[jax.ShapeDtypeStruct(*s) for s in shapes],
        compiler_params=params(),
        cost_estimate=cost(8 * count * width * part, 2 * width * (count + 4 * part)),
        interpret=INTERPRET,
    )(rows, gate_up_a, gate_up_b)


def join(near, rows, if_near, if_not):
    for value, pieces in ((1, if_near), (0, if_not)):

        @pl.when(near[0] == value)
        def _(pieces=pieces):
            rows[:, :PAIR] = pieces[0][...]
            rows[:, PAIR:] = pieces[1][...]


def backward_kernel(
    near, own, in_12, in_3, down_a, down_b, gates, back_a, back_b, rows, total
):
    k = pl.program_id(0)

    @pl.when(k == 0)
    def _():
        total[...] = jnp.zeros_like(total)

    join(near, rows, (own, in_12), (in_12, in_3))
    grads = rows[...].reshape(-1, rows.shape[2])
    for owner, down in enumerate((down_a, down_b)):
        total[owner] += lax.dot_general(
            grads, down[0], (((1,), (1,)), ((), ())), preferred_element_type=F32
        )

    @pl.when(k == pl.num_programs(0) - 1)
    def _():
        units = total.shape[2]
        for owner, back in enumerate((back_a, back_b)):
            gate, up = gates[owner, :, :units], gates[owner, :, units:]
            hidden_grad = total[owner]
            sigmoid = jax.nn.sigmoid(gate)
            back[:, :units] = (
                hidden_grad * up * sigmoid * (1.0 + gate * (1.0 - sigmoid))
            ).astype(BF16)
            back[:, units:] = (hidden_grad * (gate * sigmoid)).astype(BF16)


def backward_call(behind, near, pieces, down_a, down_b, gates):
    width = pieces[0].shape[2]
    count = 2 * YZ * PAIR
    units = down_a.shape[1]
    step = width // FORWARD_STEPS
    weight = pl.BlockSpec((1, units, step), lambda k: (0, 0, k))
    whole = lambda shape: pl.BlockSpec(shape, lambda k: (0,) * len(shape))
    return pl.pallas_call(
        after(backward_kernel, len(behind)),
        grid=(width // step,),
        in_specs=[pl.BlockSpec(memory_space=pl.ANY) for _ in behind]
        + [pl.BlockSpec(memory_space=pltpu.SMEM)]
        + [pl.BlockSpec((YZ, PAIR, step), lambda k: (0, 0, k)) for _ in pieces]
        + [weight, weight, whole(gates.shape)],
        out_specs=[whole((count, 2 * units))] * 2,
        out_shape=[jax.ShapeDtypeStruct((count, 2 * units), BF16)] * 2,
        scratch_shapes=[
            pltpu.VMEM((YZ, 2 * PAIR, step), BF16),
            pltpu.VMEM((2, count, units), F32),
        ],
        compiler_params=params(),
        cost_estimate=cost(
            4 * count * width * units, 3 * width * count + 4 * width * units + 16 * count * units
        ),
        interpret=INTERPRET,
    )(*behind, near, *pieces, down_a, down_b, gates)


def adam(gradient, first, second):
    first_new = 0.9 * first.astype(F32) + 0.1 * gradient
    second_new = 0.95 * second.astype(F32) + 0.05 * gradient * gradient
    return (first_new / (jnp.sqrt(second_new) + 1e-08)).astype(BF16)


def after(kernel, count):
    return lambda *refs: kernel(*refs[count:])


def down_kernel(
    near, hidden_a, hidden_b, own, in_12, in_3, core_12, core_x, first, second, out, rows
):
    width = rows.shape[3]
    join(near, rows.at[0], (own, in_12), (in_12, in_3))
    join(near, rows.at[1], (core_12, core_x), (core_x, core_12))
    gradient = jnp.dot(
        hidden_a[...], rows[0].reshape(-1, width), preferred_element_type=F32
    ) + jnp.dot(hidden_b[...], rows[1].reshape(-1, width), preferred_element_type=F32)
    out[0] = adam(gradient, first[0], second[0])


def down_call(behind, near, hiddens, pieces, first, second, start, units, step):
    part, count = hiddens[0].shape
    moment = pl.BlockSpec((1, part, step), lambda j: (0, 0, start + j))
    whole = pl.BlockSpec((part, count), lambda j: (0, 0))
    return pl.pallas_call(
        after(down_kernel, len(behind)),
        grid=(units,),
        in_specs=[pl.BlockSpec(memory_space=pl.ANY) for _ in behind]
        + [pl.BlockSpec(memory_space=pltpu.SMEM), whole, whole]
        + [pl.BlockSpec((YZ, PAIR, step), lambda j: (0, 0, start + j)) for _ in pieces]
        + [moment, moment],
        out_specs=pl.BlockSpec((1, part, step), lambda j: (0, 0, j)),
        out_shape=jax.ShapeDtypeStruct((1, part, units * step), BF16),
        scratch_shapes=[pltpu.VMEM((2, YZ, 2 * PAIR, step), BF16)],
        compiler_params=params(),
        cost_estimate=cost(
            4 * count * part * units * step, 2 * units * step * (3 * count + 3 * part)
        ),
        interpret=INTERPRET,
    )(*behind, near, *hiddens, *pieces, first, second)


def contract_rows(left, right):
    return lax.dot_general(left, right, (((0,), (0,)), ((), ())), preferred_element_type=F32)


def gate_up_kernel(rows_a, rows_b, back_a, back_b, first, second, out):
    inner = first.shape[3]
    gradient = contract_rows(rows_a[...], back_a[...])
    gradient = gradient + contract_rows(rows_b[...], back_b[...])
    for half in range(2):
        out[0, half] = adam(
            gradient[:, half * inner : (half + 1) * inner], first[0, half], second[0, half]
        )


def gate_up_call(behind, rows, backs, first, second, start, units, step):
    count, _ = rows[0].shape
    inner = first.shape[3]
    part = pl.BlockSpec((count, step), lambda j: (0, start + j))
    moment = pl.BlockSpec((1, 2, step, inner), lambda j: (0, 0, start + j, 0))
    whole = pl.BlockSpec((count, 2 * inner), lambda j: (0, 0))
    return pl.pallas_call(
        after(gate_up_kernel, len(behind)),
        grid=(units,),
        in_specs=[pl.BlockSpec(memory_space=pl.ANY) for _ in behind]
        + [part, part, whole, whole, moment, moment],
        out_specs=pl.BlockSpec((1, 2, step, inner), lambda j: (0, 0, j, 0)),
        out_shape=jax.ShapeDtypeStruct((1, 2, units * step, inner), BF16),
        compiler_params=params(),
        cost_estimate=cost(
            8 * count * inner * units * step, 2 * units * step * (2 * count + 6 * inner)
        ),
        interpret=INTERPRET,
    )(*behind, *rows, *backs, first, second)


def place_kernel(swapping, mine, theirs, *rest):
    out = rest[-1]

    @pl.when(swapping[0] == 1)
    def _():
        out[...] = theirs[...]

    @pl.when(swapping[0] != 1)
    def _():
        out[...] = mine[...]


def place(behind, swapping, mine, theirs, whole, shape, start, units):
    block = tuple(n // units if k == 2 else n for k, n in enumerate(mine.shape))
    at = lambda base: lambda j: (0, 0, base + j, 0)[: len(block)]
    old = behind + ([] if whole is None else [whole])
    return pl.pallas_call(
        place_kernel,
        grid=(units,),
        in_specs=[
            pl.BlockSpec(memory_space=pltpu.SMEM),
            pl.BlockSpec(block, at(0)),
            pl.BlockSpec(block, at(0)),
        ]
        + [pl.BlockSpec(memory_space=pl.ANY) for _ in old],
        out_specs=pl.BlockSpec(block, at(start)),
        out_shape=jax.ShapeDtypeStruct(shape, BF16),
        input_output_aliases={} if whole is None else {2 + len(old): 0},
        compiler_params=params(),
        cost_estimate=cost(0, 6 * mine.size),
        interpret=INTERPRET,
    )(swapping, mine, theirs, *old)


def local(
    tokens,
    cotangent,
    expert_ids,
    combine,
    slot_expert,
    swap_flag,
    w_gate_up,
    w_down,
    first_gate_up,
    first_down,
    second_gate_up,
    second_down,
):
    width = tokens.shape[1]
    core = lax.axis_index("dp") % 2
    my_slot = lax.axis_index("expert")
    side = my_slot % 2
    near = (core == side).astype(jnp.int32)
    slots = slot_expert[None, :]
    small = jnp.concatenate([expert_ids.T.astype(F32), combine.T], axis=0)
    token_goals = (token_1, token_2, token_3, token_4)

    small_core = send(small, to_core)
    cotangent_core = send(cotangent, to_core)
    tokens_in = [send(tokens, t) for t in token_goals]
    near = near.reshape(1)
    scaled = grads_call(
        core.astype(jnp.int32).reshape(1), slots, [small, small_core], [cotangent, cotangent_core]
    )
    grads_0 = over_yz(scaled)
    down_core = send(w_down, to_core)
    gate_up_core = send(w_gate_up, to_core)

    chip = jnp.concatenate([small, small_core], axis=0)
    small_a = send(chip, small_near)
    small_b = send(chip, token_3)
    small_a = jnp.where(near == 1, chip, small_a)
    picks = picks_call(side.astype(jnp.int32).reshape(1), slots, small_a, small_b)
    sent_rows = tokens_call(near, picks, [tokens] + tokens_in)
    grads_12 = send(grads_0, grad_12)
    grads_3 = send(grads_0, grad_3)
    rows_a = over_yz(sent_rows).reshape(-1, width)
    marked = marker_call(near, rows_a)
    core_12 = send(grads_12, to_core)
    other = jnp.where(near == 1, grads_0, grads_3)
    core_x = send(other, to_core)
    mine_in = [grads_0, grads_12, grads_3]
    rows_b = send(rows_a, to_core)

    swapping = swap_flag[my_slot].reshape(1)
    pending, behind, start, step = [], [], 0, width // 7
    hidden_a, hidden_other, gates = forward_call(rows_a, w_gate_up, gate_up_core)
    hidden_b = send(hidden_other, to_core)
    for units in (2, 2, 3):
        mine = down_call(
            behind,
            marked,
            (hidden_a, hidden_b),
            mine_in + [core_12, core_x],
            first_down,
            second_down,
            start,
            units,
            step,
        )
        theirs = send(mine, to_swap)
        pending.append((mine, theirs, start, units))
        behind, start = [mine], start + units
    downs = len(pending)
    back_a, back_other = backward_call(behind, marked, mine_in, w_down, down_core, gates)
    back_b = send(back_other, to_core)
    start, step = 0, width // 14
    for units in (4, 4, 4, 1, 1):
        mine = gate_up_call(
            behind,
            (rows_a, rows_b),
            (back_a, back_b),
            first_gate_up,
            second_gate_up,
            start,
            units,
            step,
        )
        theirs = send(mine, to_swap)
        pending.append((mine, theirs, start, units))
        behind, start = [mine], start + units
    whole = None
    for mine, theirs, start, units in pending[:downs]:
        whole = place([], swapping, mine, theirs, whole, w_down.shape, start, units)
    step_down, whole, behind = whole, None, [whole]
    for mine, theirs, start, units in pending[downs:]:
        whole = place(behind, swapping, mine, theirs, whole, w_gate_up.shape, start, units)
        behind = []
    return (whole, step_down)


def solution(mesh):
    return jax.shard_map(
        local,
        mesh=mesh,
        in_specs=(
            P(("dp", "expert"), None),
            P(("dp", "expert"), None),
            P(("dp", "expert"), None),
            P(("dp", "expert"), None),
            P(),
            P(),
            P("expert", None, None, "dp"),
            P("expert", "dp", None),
            P("expert", None, None, "dp"),
            P("expert", "dp", None),
            P("expert", None, None, "dp"),
            P("expert", "dp", None),
        ),
        out_specs=(P("expert", None, None, "dp"), P("expert", "dp", None)),
        check_vma=False,
    )
```

```python
import jax
import jax.numpy as jnp
from jax import lax
from jax.experimental import pallas as pl
from jax.experimental.pallas import tpu as pltpu
from jax.sharding import PartitionSpec as P


INTERPRET = False
AXES = ("dp", "expert")
YZ = 16
CAP = 12
PAIR = 2 * CAP
GATHER_STEPS = 2
FORWARD_STEPS = 2
F32 = jnp.float32
BF16 = jnp.bfloat16


def device_id(xl, c, yz, xh):
    return ((xl * 2 + c) * YZ + yz) * 2 + xh


def send(value, target):
    pairs = []
    for xl in range(2):
        for c in range(2):
            for yz in range(YZ):
                for xh in range(2):
                    goal = target(xl, c, yz, xh)
                    if goal is not None:
                        pairs.append((device_id(xl, c, yz, xh), device_id(*goal)))
    return lax.ppermute(value, AXES, pairs)


def to_core(xl, c, yz, xh):
    return (xl, 1 - c, yz, xh)


def to_swap(xl, c, yz, xh):
    return (xl, c, yz ^ (YZ // 2), xh)


def token_1(xl, c, yz, xh):
    return None if c == xh else (1 - xl, 1 - c, yz, 1 - xh)


def token_2(xl, c, yz, xh):
    return (1 - xl, c, yz, 1 - xh) if c == xh else (xl, 1 - c, yz, xh)


def token_3(xl, c, yz, xh):
    return (1 - xl, c, yz, xh) if c == xh else (xl, 1 - c, yz, 1 - xh)


def token_4(xl, c, yz, xh):
    return (xl, c, yz, 1 - xh) if c == xh else (1 - xl, 1 - c, yz, xh)


def small_near(xl, c, yz, xh):
    return None if c == xh else (1 - xl, 1 - c, yz, 1 - xh)


def grad_12(xl, c, yz, xh):
    return (1 - xl, c, yz, xh) if c == xh else (1 - xl, 1 - c, yz, 1 - xh)


def grad_3(xl, c, yz, xh):
    return None if c == xh else (xl, 1 - c, yz, 1 - xh)


def over_yz(value):
    groups = [[yz * 2 + xh for yz in range(YZ)] for xh in range(2)]
    return lax.all_to_all(value, "expert", 0, 0, axis_index_groups=groups, tiled=True)


def params(limit=None):
    return pltpu.CompilerParams(dimension_semantics=("arbitrary",), vmem_limit_bytes=limit)


def cost(flops, size):
    return pl.CostEstimate(flops=int(flops), bytes_accessed=int(size), transcendentals=0)


def row_select(side, slots_ref, small_refs):
    rows = YZ * PAIR
    tokens = small_refs[0].shape[1]
    row = lax.broadcasted_iota(jnp.int32, (rows, 1), 0).astype(F32)
    twelve = jnp.floor((row + 0.5) * (1.0 / CAP))
    place = row - twelve * CAP
    dest = jnp.floor((twelve + 0.5) * 0.5)
    block = twelve - dest * 2
    slots = slots_ref[...].astype(F32)
    lane = lax.broadcasted_iota(jnp.int32, (rows, slots.shape[1]), 1).astype(F32)
    named = jnp.sum(
        jnp.where(lane == dest * 2 + side.astype(F32), slots, 0.0), axis=1, keepdims=True
    )
    before = lax.broadcasted_iota(jnp.int32, (tokens, tokens), 0)
    after = lax.broadcasted_iota(jnp.int32, (tokens, tokens), 1)
    earlier = jnp.where(before < after, 1.0, 0.0).astype(BF16)
    picks, weight = [], jnp.zeros((rows, 1), F32)
    for b, small in enumerate(small_refs):
        first = small[0:1, :] == named
        second = small[1:2, :] == named
        hit = jnp.where(first, 1.0, jnp.where(second, 1.0, 0.0))
        position = jnp.dot(hit.astype(BF16), earlier, preferred_element_type=F32)
        wanted = jnp.where(block == float(b), place, -1.0)
        pick = jnp.where(position == wanted, hit, 0.0)
        share = jnp.where(first, small[2:3, :], small[3:4, :])
        weight = weight + jnp.sum(pick * share, axis=1, keepdims=True)
        picks.append(pick.astype(BF16))
    return picks, weight


def picks_kernel(side, slots, near_small, far_small, out):
    tokens = near_small.shape[1]
    for group, small in enumerate((near_small[...], far_small[...])):
        half = small.shape[0] // 2
        found, _ = row_select(side[0], slots, (small[:half], small[half:]))
        out[group, :, :tokens] = found[0]
        out[group, :, tokens:] = found[1]


def picks_call(side, slots, near_small, far_small):
    return pl.pallas_call(
        picks_kernel,
        in_specs=[pl.BlockSpec(memory_space=pltpu.SMEM)]
        + [pl.BlockSpec(memory_space=pltpu.VMEM)] * 3,
        out_specs=pl.BlockSpec(memory_space=pltpu.VMEM),
        out_shape=jax.ShapeDtypeStruct((2, YZ * PAIR, 2 * near_small.shape[1]), BF16),
        cost_estimate=cost(10**8, 10**6),
        interpret=INTERPRET,
    )(side, slots, near_small, far_small)


def grads_kernel(side, slots, small_a, small_b, data_a, data_b, out, picks, weights, both):
    count = data_a.shape[0]

    @pl.when(pl.program_id(0) == 0)
    def _():
        found, weight = row_select(side[0], slots, (small_a, small_b))
        picks[:, :count] = found[0]
        picks[:, count:] = found[1]
        weights[...] = weight

    both[:count] = data_a[...]
    both[count:] = data_b[...]
    rows = jnp.dot(picks[...], both[...], preferred_element_type=F32)
    rows = (rows * weights[...]).astype(BF16)
    for yz in range(YZ):
        out[yz] = rows[yz * PAIR : (yz + 1) * PAIR]


def grads_call(side, slots, smalls, data):
    count, width = data[0].shape
    step = width // GATHER_STEPS
    whole = lambda shape: pl.BlockSpec(shape, lambda j: (0,) * len(shape))
    rows = YZ * PAIR
    return pl.pallas_call(
        grads_kernel,
        grid=(width // step,),
        in_specs=[pl.BlockSpec(memory_space=pltpu.SMEM), whole(slots.shape)]
        + [whole(s.shape) for s in smalls]
        + [pl.BlockSpec((count, step), lambda j: (0, j)) for _ in data],
        out_specs=pl.BlockSpec((YZ, PAIR, step), lambda j: (0, 0, j)),
        out_shape=jax.ShapeDtypeStruct((YZ, PAIR, width), BF16),
        scratch_shapes=[
            pltpu.VMEM((rows, 2 * count), BF16),
            pltpu.VMEM((rows, 1), F32),
            pltpu.VMEM((2 * count, step), BF16),
        ],
        compiler_params=params(),
        cost_estimate=cost(4 * rows * count * width, 2 * width * (2 * count + rows)),
        interpret=INTERPRET,
    )(side, slots, *smalls, *data)


def tokens_kernel(near, picks, own, data_a, data_b, data_c, data_d, out, both):
    count = own.shape[0]

    @pl.when(near[0] == 1)
    def _():
        both[:count] = own[...]

    @pl.when(near[0] != 1)
    def _():
        both[:count] = data_a[...]

    both[count : 2 * count] = data_b[...]
    both[2 * count : 3 * count] = data_c[...]
    both[3 * count :] = data_d[...]
    for group in range(2):
        rows = jnp.dot(
            picks[group],
            both[2 * group * count : 2 * (group + 1) * count],
            preferred_element_type=F32,
        ).astype(BF16)
        for yz in range(YZ):
            out[yz, group * PAIR : (group + 1) * PAIR] = rows[yz * PAIR : (yz + 1) * PAIR]


def tokens_call(near, picks, data):
    count, width = data[0].shape
    step = width // GATHER_STEPS
    rows = YZ * PAIR
    return pl.pallas_call(
        tokens_kernel,
        grid=(width // step,),
        in_specs=[
            pl.BlockSpec(memory_space=pltpu.SMEM),
            pl.BlockSpec(picks.shape, lambda j: (0, 0, 0)),
        ]
        + [pl.BlockSpec((count, step), lambda j: (0, j)) for _ in data],
        out_specs=pl.BlockSpec((YZ, 2 * PAIR, step), lambda j: (0, 0, j)),
        out_shape=jax.ShapeDtypeStruct((YZ, 2 * PAIR, width), BF16),
        scratch_shapes=[pltpu.VMEM((4 * count, step), BF16)],
        compiler_params=params(),
        cost_estimate=cost(8 * rows * count * width, 2 * width * (5 * count + 2 * rows)),
        interpret=INTERPRET,
    )(near, picks, *data)


def marker_kernel(near, rows, out):
    out[0] = near[0]


def marker_call(near, rows):
    return pl.pallas_call(
        marker_kernel,
        in_specs=[
            pl.BlockSpec(memory_space=pltpu.SMEM),
            pl.BlockSpec(memory_space=pl.ANY),
        ],
        out_specs=pl.BlockSpec(memory_space=pltpu.SMEM),
        out_shape=jax.ShapeDtypeStruct((1,), jnp.int32),
        interpret=INTERPRET,
    )(near, rows)


def forward_kernel(rows, gate_up_a, gate_up_b, hidden_a, hidden_b, total):
    k = pl.program_id(0)

    @pl.when(k == 0)
    def _():
        total[...] = jnp.zeros_like(total)

    for owner, gate_up in enumerate((gate_up_a, gate_up_b)):
        weight = jnp.concatenate([gate_up[0, 0], gate_up[0, 1]], axis=1)
        total[owner] += jnp.dot(rows[...], weight, preferred_element_type=F32)

    @pl.when(k == pl.num_programs(0) - 1)
    def _():
        part = hidden_a.shape[0]
        for owner, hidden_t in enumerate((hidden_a, hidden_b)):
            gate, up = total[owner, :, :part], total[owner, :, part:]
            hidden_t[...] = jnp.transpose(gate * jax.nn.sigmoid(gate) * up).astype(BF16)


def forward_call(rows, gate_up_a, gate_up_b):
    count, width = rows.shape
    part = gate_up_a.shape[3]
    step = width // FORWARD_STEPS
    weight = pl.BlockSpec((1, 2, step, part), lambda k: (0, 0, k, 0))
    whole = lambda shape: pl.BlockSpec(shape, lambda k: (0,) * len(shape))
    shapes = [((part, count), BF16), ((part, count), BF16), ((2, count, 2 * part), F32)]
    return pl.pallas_call(
        forward_kernel,
        grid=(width // step,),
        in_specs=[pl.BlockSpec((count, step), lambda k: (0, k)), weight, weight],
        out_specs=[whole(s) for s, _ in shapes],
        out_shape=[jax.ShapeDtypeStruct(*s) for s in shapes],
        compiler_params=params(67_000_000),
        cost_estimate=cost(8 * count * width * part, 2 * width * (count + 4 * part)),
        interpret=INTERPRET,
    )(rows, gate_up_a, gate_up_b)


def join(near, rows, if_near, if_not):
    for value, pieces in ((1, if_near), (0, if_not)):

        @pl.when(near[0] == value)
        def _(pieces=pieces):
            rows[:, :PAIR] = pieces[0][...]
            rows[:, PAIR:] = pieces[1][...]


def backward_kernel(
    near, own, in_12, in_3, down_a, down_b, gates, back_a, back_b, rows, total
):
    k = pl.program_id(0)

    @pl.when(k == 0)
    def _():
        total[...] = jnp.zeros_like(total)

    join(near, rows, (own, in_12), (in_12, in_3))
    grads = rows[...].reshape(-1, rows.shape[2])
    for owner, down in enumerate((down_a, down_b)):
        total[owner] += lax.dot_general(
            grads, down[0], (((1,), (1,)), ((), ())), preferred_element_type=F32
        )

    @pl.when(k == pl.num_programs(0) - 1)
    def _():
        units = total.shape[2]
        for owner, back in enumerate((back_a, back_b)):
            gate, up = gates[owner, :, :units], gates[owner, :, units:]
            hidden_grad = total[owner]
            sigmoid = jax.nn.sigmoid(gate)
            back[:, :units] = (
                hidden_grad * up * sigmoid * (1.0 + gate * (1.0 - sigmoid))
            ).astype(BF16)
            back[:, units:] = (hidden_grad * (gate * sigmoid)).astype(BF16)


def backward_call(behind, near, pieces, down_a, down_b, gates):
    width = pieces[0].shape[2]
    count = 2 * YZ * PAIR
    units = down_a.shape[1]
    step = width // FORWARD_STEPS
    weight = pl.BlockSpec((1, units, step), lambda k: (0, 0, k))
    whole = lambda shape: pl.BlockSpec(shape, lambda k: (0,) * len(shape))
    return pl.pallas_call(
        after(backward_kernel, len(behind)),
        grid=(width // step,),
        in_specs=[pl.BlockSpec(memory_space=pl.ANY) for _ in behind]
        + [pl.BlockSpec(memory_space=pltpu.SMEM)]
        + [pl.BlockSpec((YZ, PAIR, step), lambda k: (0, 0, k)) for _ in pieces]
        + [weight, weight, whole(gates.shape)],
        out_specs=[whole((count, 2 * units))] * 2,
        out_shape=[jax.ShapeDtypeStruct((count, 2 * units), BF16)] * 2,
        scratch_shapes=[
            pltpu.VMEM((YZ, 2 * PAIR, step), BF16),
            pltpu.VMEM((2, count, units), F32),
        ],
        compiler_params=params(),
        cost_estimate=cost(
            4 * count * width * units, 3 * width * count + 4 * width * units + 16 * count * units
        ),
        interpret=INTERPRET,
    )(*behind, near, *pieces, down_a, down_b, gates)


def adam(gradient, first, second):
    first_new = 0.9 * first.astype(F32) + 0.1 * gradient
    second_new = 0.95 * second.astype(F32) + 0.05 * gradient * gradient
    return (first_new / (jnp.sqrt(second_new) + 1e-08)).astype(BF16)


def after(kernel, count):
    return lambda *refs: kernel(*refs[count:])


def down_kernel(
    near, hidden_a, hidden_b, own, in_12, in_3, core_12, core_x, first, second, out, rows
):
    width = rows.shape[3]
    join(near, rows.at[0], (own, in_12), (in_12, in_3))
    join(near, rows.at[1], (core_12, core_x), (core_x, core_12))
    gradient = jnp.dot(
        hidden_a[...], rows[0].reshape(-1, width), preferred_element_type=F32
    ) + jnp.dot(hidden_b[...], rows[1].reshape(-1, width), preferred_element_type=F32)
    out[0] = adam(gradient, first[0], second[0])


def down_call(behind, near, hiddens, pieces, first, second, start, units, step):
    part, count = hiddens[0].shape
    moment = pl.BlockSpec((1, part, step), lambda j: (0, 0, start + j))
    whole = pl.BlockSpec((part, count), lambda j: (0, 0))
    return pl.pallas_call(
        after(down_kernel, len(behind)),
        grid=(units,),
        in_specs=[pl.BlockSpec(memory_space=pl.ANY) for _ in behind]
        + [pl.BlockSpec(memory_space=pltpu.SMEM), whole, whole]
        + [pl.BlockSpec((YZ, PAIR, step), lambda j: (0, 0, start + j)) for _ in pieces]
        + [moment, moment],
        out_specs=pl.BlockSpec((1, part, step), lambda j: (0, 0, j)),
        out_shape=jax.ShapeDtypeStruct((1, part, units * step), BF16),
        scratch_shapes=[pltpu.VMEM((2, YZ, 2 * PAIR, step), BF16)],
        compiler_params=params(),
        cost_estimate=cost(
            4 * count * part * units * step, 2 * units * step * (3 * count + 3 * part)
        ),
        interpret=INTERPRET,
    )(*behind, near, *hiddens, *pieces, first, second)


def contract_rows(left, right):
    return lax.dot_general(left, right, (((0,), (0,)), ((), ())), preferred_element_type=F32)


def gate_up_kernel(rows_a, rows_b, back_a, back_b, first, second, out):
    inner = first.shape[3]
    gradient = contract_rows(rows_a[...], back_a[...])
    gradient = gradient + contract_rows(rows_b[...], back_b[...])
    for half in range(2):
        out[0, half] = adam(
            gradient[:, half * inner : (half + 1) * inner], first[0, half], second[0, half]
        )


def gate_up_call(behind, rows, backs, first, second, start, units, step):
    count, _ = rows[0].shape
    inner = first.shape[3]
    part = pl.BlockSpec((count, step), lambda j: (0, start + j))
    moment = pl.BlockSpec((1, 2, step, inner), lambda j: (0, 0, start + j, 0))
    whole = pl.BlockSpec((count, 2 * inner), lambda j: (0, 0))
    return pl.pallas_call(
        after(gate_up_kernel, len(behind)),
        grid=(units,),
        in_specs=[pl.BlockSpec(memory_space=pl.ANY) for _ in behind]
        + [part, part, whole, whole, moment, moment],
        out_specs=pl.BlockSpec((1, 2, step, inner), lambda j: (0, 0, j, 0)),
        out_shape=jax.ShapeDtypeStruct((1, 2, units * step, inner), BF16),
        compiler_params=params(),
        cost_estimate=cost(
            8 * count * inner * units * step, 2 * units * step * (2 * count + 6 * inner)
        ),
        interpret=INTERPRET,
    )(*behind, *rows, *backs, first, second)


def place_kernel(swapping, mine, theirs, *rest):
    out = rest[-1]

    @pl.when(swapping[0] == 1)
    def _():
        out[...] = theirs[...]

    @pl.when(swapping[0] != 1)
    def _():
        out[...] = mine[...]


def place(behind, swapping, mine, theirs, whole, shape, start, units):
    block = tuple(n // units if k == 2 else n for k, n in enumerate(mine.shape))
    at = lambda base: lambda j: (0, 0, base + j, 0)[: len(block)]
    old = behind + ([] if whole is None else [whole])
    return pl.pallas_call(
        place_kernel,
        grid=(units,),
        in_specs=[
            pl.BlockSpec(memory_space=pltpu.SMEM),
            pl.BlockSpec(block, at(0)),
            pl.BlockSpec(block, at(0)),
        ]
        + [pl.BlockSpec(memory_space=pl.ANY) for _ in old],
        out_specs=pl.BlockSpec(block, at(start)),
        out_shape=jax.ShapeDtypeStruct(shape, BF16),
        input_output_aliases={} if whole is None else {2 + len(old): 0},
        compiler_params=params(),
        cost_estimate=cost(0, 6 * mine.size),
        interpret=INTERPRET,
    )(swapping, mine, theirs, *old)


def local(
    tokens,
    cotangent,
    expert_ids,
    combine,
    slot_expert,
    swap_flag,
    w_gate_up,
    w_down,
    first_gate_up,
    first_down,
    second_gate_up,
    second_down,
):
    width = tokens.shape[1]
    core = lax.axis_index("dp") % 2
    my_slot = lax.axis_index("expert")
    side = my_slot % 2
    near = (core == side).astype(jnp.int32)
    slots = slot_expert[None, :]
    small = jnp.concatenate([expert_ids.T.astype(F32), combine.T], axis=0)
    token_goals = (token_1, token_2, token_3, token_4)

    small_core = send(small, to_core)
    cotangent_core = send(cotangent, to_core)
    tokens_in = [send(tokens, t) for t in token_goals]
    near = near.reshape(1)
    scaled = grads_call(
        core.astype(jnp.int32).reshape(1), slots, [small, small_core], [cotangent, cotangent_core]
    )
    grads_0 = over_yz(scaled)
    down_core = send(w_down, to_core)
    gate_up_core = send(w_gate_up, to_core)

    chip = jnp.concatenate([small, small_core], axis=0)
    small_a = send(chip, small_near)
    small_b = send(chip, token_3)
    small_a = jnp.where(near == 1, chip, small_a)
    picks = picks_call(side.astype(jnp.int32).reshape(1), slots, small_a, small_b)
    sent_rows = tokens_call(near, picks, [tokens] + tokens_in)
    grads_12 = send(grads_0, grad_12)
    grads_3 = send(grads_0, grad_3)
    rows_a = over_yz(sent_rows).reshape(-1, width)
    marked = marker_call(near, rows_a)
    core_12 = send(grads_12, to_core)
    other = jnp.where(near == 1, grads_0, grads_3)
    core_x = send(other, to_core)
    mine_in = [grads_0, grads_12, grads_3]
    rows_b = send(rows_a, to_core)

    swapping = swap_flag[my_slot].reshape(1)
    pending, behind, start, step = [], [], 0, width // 7
    hidden_a, hidden_other, gates = forward_call(rows_a, w_gate_up, gate_up_core)
    hidden_b = send(hidden_other, to_core)
    for units in (2, 2, 3):
        mine = down_call(
            behind,
            marked,
            (hidden_a, hidden_b),
            mine_in + [core_12, core_x],
            first_down,
            second_down,
            start,
            units,
            step,
        )
        theirs = send(mine, to_swap)
        pending.append((mine, theirs, start, units))
        behind, start = [mine], start + units
    downs = len(pending)
    back_a, back_other = backward_call(behind, marked, mine_in, w_down, down_core, gates)
    back_b = send(back_other, to_core)
    start, step = 0, width // 14
    for units in (4, 4, 4, 1, 1):
        mine = gate_up_call(
            behind,
            (rows_a, rows_b),
            (back_a, back_b),
            first_gate_up,
            second_gate_up,
            start,
            units,
            step,
        )
        theirs = send(mine, to_swap)
        pending.append((mine, theirs, start, units))
        behind, start = [mine], start + units
    whole = None
    for mine, theirs, start, units in pending[:downs]:
        whole = place([], swapping, mine, theirs, whole, w_down.shape, start, units)
    step_down, whole, behind = whole, None, [whole]
    for mine, theirs, start, units in pending[downs:]:
        whole = place(behind, swapping, mine, theirs, whole, w_gate_up.shape, start, units)
        behind = []
    return (whole, step_down)


def solution(mesh):
    return jax.shard_map(
        local,
        mesh=mesh,
        in_specs=(
            P(("dp", "expert"), None),
            P(("dp", "expert"), None),
            P(("dp", "expert"), None),
            P(("dp", "expert"), None),
            P(),
            P(),
            P("expert", None, None, "dp"),
            P("expert", "dp", None),
            P("expert", None, None, "dp"),
            P("expert", "dp", None),
            P("expert", None, None, "dp"),
            P("expert", "dp", None),
        ),
        out_specs=(P("expert", None, None, "dp"), P("expert", "dp", None)),
        check_vma=False,
    )
```
